32 devices in a mesh: rel: 2 (over x), ent: 16 (over z, y, core).
Axes of the slice: x: 2, y: 2, z: 4, core: 2. Of those that a mesh axis runs over, the one named last changes fastest.
Arguments:
- state: bfloat16 [4096, 1024], P('ent', 'rel'), may hold values from -4 to 4
- rel_weight: bfloat16 [24, 1024, 1024], P('rel', 'ent'), may hold values from -0.0390625 to 0.0390625
- gate_weight: bfloat16 [1024, 1024], P(None, 'rel'), may hold values from -0.1875 to 0.1875
- gate_bias: float32 [1024], P('rel'), may hold values from -4 to 4
- update_bias: float32 [1024], P('rel'), may hold values from -3 to 3
- tile_values: bfloat16 [2, 256, 128, 128], P('rel', 'ent'), may hold values from 0 to 0.119628906
- tile_index: int32 [2, 3, 256], P('rel', None, 'ent'), may hold values from 0 to 31, as said below
- tile_count: int32 [2, 16], P('rel', 'ent'), may hold values from 1 to 16, as said below
Outputs:
- new_state: bfloat16 [4096, 1024], P('ent', 'rel')
The draws below stay inside these ranges and needn't reach their ends.
Inputs may be any that keep to these rules, and one draw needn't show every extreme that they name: `tile_index`: row 0 names a source tile of the whole graph, row 1 a destination tile of the partition that owns the slot (below 2), row 2 a relation within the group (below 12). `tile_count`: slots of a partition at or past its count are padding; in every group some partition fills all 16 slots.
All inputs are finite; a program needn't handle non-finite values.
Results may differ from the reference program's by a relative error of at most 0.0065.
Values may be sent and summed in bfloat16 or wider, within the bound.
No kernel may reach another device: no remote copies, remote signals or barrier semaphores. Data moves between devices by JAX's collectives and lax.ppermute only.
A program may use at most 128 MiB of HBM per device.

```python
import jax
import jax.numpy as jnp
from jax import lax

H = 1024
RELS = 24
TILE = 128
LAYERS = 1
ENT_DEV = 256
SLOTS = 16
GROUPS = 2
PARTS_SIZE = 16
NODES = 4096
LISTED = 256
N_REL = 2
N_ENT = 16


def draw_tile_index(key, part):
    keys = jax.random.split(jax.random.fold_in(key, 11), 3)
    source = jax.random.randint(keys[0], (GROUPS, LISTED), 0, NODES // TILE, dtype=jnp.int32)
    target = jax.random.randint(keys[1], (GROUPS, LISTED), 0, ENT_DEV // TILE, dtype=jnp.int32)
    relation = jax.random.randint(keys[2], (GROUPS, LISTED), 0, RELS // GROUPS, dtype=jnp.int32)
    return jnp.stack([source, target, relation], axis=1)


def draw_tile_count(key, part):
    keys = jax.random.split(jax.random.fold_in(key, 23), 2)
    counts = jax.random.randint(keys[0], (GROUPS, PARTS_SIZE), 1, SLOTS + 1, dtype=jnp.int32)
    chosen = jax.random.randint(keys[1], (GROUPS, 1), 0, PARTS_SIZE, dtype=jnp.int32)
    spots = jnp.arange(PARTS_SIZE, dtype=jnp.int32)[None, :] == chosen
    return jnp.where(spots, SLOTS, counts).astype(jnp.int32)


def block_levels(rng, dims, cuts, low, high):
    loudness = 1.0
    for dim, parts in cuts:
        heights = jax.random.uniform(jax.random.fold_in(jax.random.fold_in(rng, 6), dim), (parts,), jnp.float32, low / len(cuts), high / len(cuts))
        loudness = loudness * jnp.repeat(jnp.exp(heights), dims[dim] // parts).reshape((-1,) + (1,) * (len(dims) - 1 - dim))
    return loudness


def bell_draw(own_key, dims, scale, bound, shards=(), held_as=jnp.bfloat16):
    drawn = jax.random.normal(own_key, dims, jnp.float32) * scale
    if len(shards) > 0:
        drawn = block_levels(own_key, dims, shards, -0.22, 0.18) * drawn
    return jnp.clip(drawn, min=-bound, max=bound).astype(held_as)


def setup_inputs(seed: int = 0) -> dict:
    key_list = jax.random.split(jax.random.key(seed), 9)
    state = bell_draw(key_list[0], (NODES, H), 1.0, 4.0, ((0, 16), (1, 2)))
    rel_weight = bell_draw(key_list[1], (RELS, H, H), (H * RELS) ** -0.5, 0.0390625, ((0, 2), (1, 16)))
    gate_weight = bell_draw(key_list[2], (H, H), H ** -0.5, 0.1875, ((1, 2),))
    gate_bias = bell_draw(key_list[3], (H,), 1.0, 4.0, ((0, 2),), jnp.float32)
    update_bias = bell_draw(key_list[4], (H,), 0.7, 3.0, ((0, 2),), jnp.float32)
    tile_values = jnp.clip(0.119628906 * jax.random.uniform(key_list[5], (GROUPS, LISTED, TILE, TILE), jnp.float32) ** block_levels(key_list[5], (GROUPS, LISTED, TILE, TILE), ((0, 2), (1, 16)), -0.2, 0.2), 0.0, 0.119628906).astype(jnp.bfloat16)
    tile_index = draw_tile_index(jax.random.fold_in(key_list[8], 71), 0)
    tile_count = draw_tile_count(jax.random.fold_in(key_list[8], 71), 0)
    return {"state": state, "rel_weight": rel_weight, "gate_weight": gate_weight, "gate_bias": gate_bias, "update_bias": update_bias, "tile_values": tile_values, "tile_index": tile_index, "tile_count": tile_count}


def aggregate_tiles(hidden, values, listing, live_total, rel_dev, per_tile):
    features = hidden.shape[1]
    sources = hidden.reshape(-1, TILE, features)[listing[0]]
    product = jnp.einsum("sij,sjh->sih", values.astype(jnp.float32), sources.astype(jnp.float32))
    slot_ids = jnp.arange(listing.shape[1], dtype=jnp.int32)
    live_mask = (slot_ids < live_total).astype(jnp.float32)
    target = listing[1] * rel_dev + listing[2]
    classes = jnp.arange(per_tile * rel_dev, dtype=jnp.int32)
    select = (target[:, None] == classes[None, :]).astype(jnp.float32) * live_mask[:, None]
    summed = jnp.einsum("sk,sih->kih", select, product, precision=lax.Precision.HIGHEST)
    return summed.astype(jnp.bfloat16).reshape(per_tile, rel_dev, TILE, features)


def reference(state, rel_weight, gate_weight, gate_bias, update_bias, tile_values, tile_index, tile_count):
    rel_dev = RELS // N_REL
    per_tile = ENT_DEV // TILE
    hidden = state
    for layer_num in range(LAYERS):
        def partition(part_num):
            summed = jnp.zeros((ENT_DEV, H), jnp.float32)
            for group in range(N_REL):
                first_slot = part_num * SLOTS
                values = lax.dynamic_slice_in_dim(tile_values[group], first_slot, SLOTS, 0)
                listing = lax.dynamic_slice_in_dim(tile_index[group], first_slot, SLOTS, 1)
                live_total = tile_count[group][part_num]
                aggregate = aggregate_tiles(hidden, values, listing, live_total, rel_dev, per_tile)
                weights = rel_weight[group * rel_dev:(group + 1) * rel_dev].astype(jnp.float32)
                term = jnp.einsum("drih,rhk->dik", aggregate.astype(jnp.float32), weights)
                summed = summed + term.reshape(ENT_DEV, H)
            return summed

        message = lax.map(partition, jnp.arange(N_ENT, dtype=jnp.int32)).reshape(NODES, H)
        gate_open = jax.nn.sigmoid(jnp.dot(hidden, gate_weight, preferred_element_type=jnp.float32) + gate_bias)
        update = jnp.tanh(message + update_bias)
        hidden = ((1.0 - gate_open) * hidden.astype(jnp.float32) + gate_open * update).astype(jnp.bfloat16)
    return hidden
```

```python
import functools

import jax
import jax.numpy as jnp
from jax import lax
from jax.experimental import pallas as pl
from jax.experimental.pallas import tpu as pltpu
from jax.sharding import PartitionSpec as P


F32 = jnp.float32
BF16 = jnp.bfloat16
ANY = pl.BlockSpec(memory_space=pl.ANY)


def xor_swap(value, axis, size, bit):
    return lax.ppermute(value, axis, [(i, i ^ bit) for i in range(size)])


def products_kernel(chunks, members, table, counts, *refs):
    states = refs[:members]
    tiles = refs[members:members + chunks]
    out = refs[members + chunks]
    held, lists, state_sem, tile_sem = refs[members + chunks + 1:]
    slots = tiles[0].shape[0]
    per_member = states[0].shape[0]
    copies = [
        pltpu.make_async_copy(ref, held.at[pl.ds(i * per_member, per_member)], state_sem.at[i])
        for i, ref in enumerate(states)
    ]
    loads = [pltpu.make_async_copy(ref, lists.at[j], tile_sem.at[j]) for j, ref in enumerate(tiles)]
    for copy in copies + loads:
        copy.start()
    for copy in copies:
        copy.wait()
    for j in range(chunks):
        loads[j].wait()

        def step(s, _, j=j):
            rows = held[table[0, j * slots + s]]
            made = jnp.dot(lists[j, s], rows, preferred_element_type=F32)
            out[j, s] = made.astype(BF16)
            return 0

        lax.fori_loop(0, counts[j], step, 0)


def messages_kernel(chunks, members, column_cut, table, counts, home, made, *refs):
    weights = refs[:members]
    out = refs[members]
    held, acc, sem = refs[members + 1:]
    slots = made.shape[1]
    block = weights[0].shape[1]
    per_tile = acc.shape[0]
    copies = []
    for i, ref in enumerate(weights):
        start = pl.multiple_of(lax.bitwise_xor(home[0], i) * block, block)
        copies.append(pltpu.make_async_copy(ref, held.at[:, pl.ds(start, block), :], sem.at[i]))
    for copy in copies:
        copy.start()
    for copy in copies:
        copy.wait()
    features = out.shape[-1]
    for j in range(chunks):
        acc[...] = jnp.zeros_like(acc)

        def step(s, _, j=j):
            target = table[1, j * slots + s]
            relation = table[2, j * slots + s]
            rows = made[j, s]
            for c in range(0, features, column_cut):
                acc[target, :, c:c + column_cut] += jnp.dot(
                    rows, held[relation, :, c:c + column_cut], preferred_element_type=F32
                )
            return 0

        lax.fori_loop(0, counts[j], step, 0)
        for t in range(per_tile):
            out[j, t] = acc[t].astype(out.dtype)


def shards(
    n_rel, n_ent, chunks, state, rel_weight, gate_weight, gate_bias, update_bias,
    tile_values, tile_index, tile_count
):
    members = n_ent // chunks
    rel_dev, block, features = rel_weight.shape
    ent_dev, own_features = state.shape
    tile_rows = tile_values.shape[-1]
    slots = tile_values.shape[1]
    per_tile = ent_dev // tile_rows
    width = features // chunks
    rel = lax.axis_index("rel")
    ent = lax.axis_index("ent")
    part, member = ent // members, ent % members
    bits = [1 << b for b in range(members.bit_length() - 1)]

    def shift(value, d):
        perm = [
            (q * members + m, ((q + d) % chunks) * members + m)
            for q in range(chunks)
            for m in range(members)
        ]
        return lax.ppermute(value, "ent", perm)

    def gather_members(value):
        held = [value]
        for bit in reversed(bits):
            held = held + [xor_swap(v, "ent", n_ent, bit) for v in held]
        order = []
        for bit in reversed(bits):
            order = (order or [0]) + [o | bit for o in (order or [0])]
        return [held[order.index(i)] for i in range(members)] if bits else held

    values = tile_values[0]
    note = jnp.zeros((16, tile_rows), BF16)
    note = note.at[:3, :slots].set(tile_index[0].astype(BF16))
    note = note.at[3, :1].set(tile_count[0].astype(BF16))
    tiles = [values] + [shift(values, d) for d in range(1, chunks)]
    notes = [note] + [shift(note, d) for d in range(1, chunks)]

    halves = [state]
    for r in range(1, n_rel):
        halves.append(xor_swap(state, "rel", n_rel, r))
    stacked = jnp.stack(halves)

    def columns_of(q):
        per_half = chunks // n_rel
        owner = lax.bitwise_xor(q // per_half, rel)
        return lax.dynamic_slice(
            stacked, (owner, 0, (q % per_half) * width), (1, ent_dev, width)
        )[0]

    pieces = [columns_of(part)]
    for d in range(1, chunks):
        pieces.append(shift(columns_of((part + d) % chunks), d))
    own = jnp.stack(pieces).reshape(chunks * per_tile, tile_rows, width)
    states = gather_members(own)
    weights = gather_members(rel_weight)

    notes = jnp.stack(notes).astype(jnp.int32)
    counts = notes[:, 3, 0]
    source, target, relation = notes[:, 0, :slots], notes[:, 1, :slots], notes[:, 2, :slots]
    owner = source // per_tile
    place = lax.bitwise_xor(owner % members, member) * chunks
    place = (place + (part - owner // members) % chunks) * per_tile + source % per_tile
    table = jnp.stack([place.reshape(-1), target.reshape(-1), relation.reshape(-1)])

    smem = pl.BlockSpec(memory_space=pltpu.SMEM)
    vmem = pl.BlockSpec(memory_space=pltpu.VMEM)
    made = pl.pallas_call(
        functools.partial(products_kernel, chunks, members),
        out_shape=jax.ShapeDtypeStruct((chunks, slots, tile_rows, width), BF16),
        in_specs=[smem, smem] + [ANY] * (members + chunks),
        out_specs=vmem,
        scratch_shapes=[
            pltpu.VMEM((members * chunks * per_tile, tile_rows, width), BF16),
            pltpu.VMEM((chunks, slots, tile_rows, tile_rows), BF16),
            pltpu.SemaphoreType.DMA((members,)),
            pltpu.SemaphoreType.DMA((chunks,)),
        ],
        cost_estimate=pl.CostEstimate(
            flops=2 * chunks * slots * tile_rows * tile_rows * width,
            bytes_accessed=2 * (n_ent * ent_dev * width + chunks * slots * tile_rows * (tile_rows + width)),
            transcendentals=0,
        ),
        name="products",
    )(table, counts, *states, *tiles)
    partial = pl.pallas_call(
        functools.partial(messages_kernel, chunks, members, min(512, features)),
        out_shape=jax.ShapeDtypeStruct((chunks, per_tile, tile_rows, features), F32),
        in_specs=[smem, smem, smem, vmem] + [ANY] * members,
        out_specs=vmem,
        scratch_shapes=[
            pltpu.VMEM((rel_dev, width, features), BF16),
            pltpu.VMEM((per_tile, tile_rows, features), F32),
            pltpu.SemaphoreType.DMA((members,)),
        ],
        cost_estimate=pl.CostEstimate(
            flops=2 * chunks * slots * tile_rows * width * features,
            bytes_accessed=2 * rel_dev * width * features,
            transcendentals=0,
        ),
        name="messages",
    )(table, counts, member.reshape(1), made, *weights)
    partial = partial.reshape(chunks, ent_dev, features)

    def feature_block(value, r):
        return lax.dynamic_slice_in_dim(value, r * own_features, own_features, 1)

    message = None
    for j in reversed(range(chunks)):
        term = feature_block(partial[j], rel)
        for r in range(1, n_rel):
            sent = feature_block(partial[j], lax.bitwise_xor(rel, r)).astype(BF16)
            term = term + xor_swap(sent, "rel", n_rel, r).astype(F32)
        if j > 0:
            term = shift(term.astype(BF16), chunks - j).astype(F32)
        message = term if message is None else message + term

    gate = gate_bias
    for r in range(n_rel):
        rows = lax.dynamic_slice_in_dim(
            gate_weight, lax.bitwise_xor(rel, r) * own_features, own_features, 0
        )
        gate = gate + jnp.dot(halves[r], rows, preferred_element_type=F32)
    gate_open = jax.nn.sigmoid(gate)
    update = jnp.tanh(message + update_bias)
    return ((1.0 - gate_open) * state.astype(F32) + gate_open * update).astype(BF16)


def solution(mesh):
    n_rel, n_ent = mesh.shape["rel"], mesh.shape["ent"]
    chunks = max(4, n_rel)
    in_specs = (
        P("ent", "rel"),
        P("rel", "ent", None),
        P(None, "rel"),
        P("rel"),
        P("rel"),
        P("rel", "ent", None, None),
        P("rel", None, "ent"),
        P("rel", "ent"),
    )
    return jax.shard_map(
        functools.partial(shards, n_rel, n_ent, chunks),
        mesh=mesh, in_specs=in_specs, out_specs=P("ent", "rel"), check_vma=False,
    )
```

```python
import functools

import jax
import jax.numpy as jnp
from jax import lax
from jax.experimental import pallas as pl
from jax.experimental.pallas import tpu as pltpu
from jax.sharding import PartitionSpec as P


F32 = jnp.float32
BF16 = jnp.bfloat16
ANY = pl.BlockSpec(memory_space=pl.ANY)
SMEM = pl.BlockSpec(memory_space=pltpu.SMEM)
VMEM = pl.BlockSpec(memory_space=pltpu.VMEM)
GROUP = 4
NOTE_ROWS = 16


def swap(value, axis, size, bit):
    return lax.ppermute(value, axis, [(i, i ^ bit) for i in range(size)])


def pack_kernel(n_rel, where, note, *refs):
    halves, outs = refs[:n_rel], refs[n_rel:]
    rows, width = halves[0].shape[0], outs[0].shape[1]
    for j, out in enumerate(outs):
        start = pl.multiple_of(where[1, j], width)
        for r, half in enumerate(halves):

            @pl.when(where[0, j] == r)
            def _(half=half, out=out, start=start):
                out[:rows] = half[:, pl.ds(start, width)]

        if out.shape[0] > rows:
            out[rows:] = note[...]


def gate_kernel(n_rel, rel, weight, bias, *refs):
    halves, out = refs[:n_rel], refs[n_rel]
    depth = halves[0].shape[1]
    total = jnp.zeros(out.shape, F32) + bias[...]
    for r, half in enumerate(halves):
        start = pl.multiple_of(lax.bitwise_xor(rel[0], r) * depth, depth)
        total += jnp.dot(half[...], weight[pl.ds(start, depth), :], preferred_element_type=F32)
    out[...] = jax.nn.sigmoid(total)


def messages_kernel(plan, table, counts, home, *refs):
    js, members, tile_ways, n_weights, n_rel, tile_rows = plan
    states, refs = refs[:members], refs[members:]
    n_tiles = sum(len(ways) for ways in tile_ways)
    tiles, refs = refs[:n_tiles], refs[n_tiles:]
    weights, refs = refs[:n_weights], refs[n_weights:]
    outs, refs = refs[:len(js) * n_rel], refs[len(js) * n_rel:]
    rows_held, lists, made, held, acc, state_sem, tile_sem, weight_sem = refs
    slots = lists.shape[1]
    per_tile = acc.shape[0] - 1
    features = acc.shape[-1]
    own = features // n_rel
    block = weights[0].shape[1]
    per_member = states[0].shape[0]

    loads = []
    for i, ref in enumerate(states):
        loads.append(
            pltpu.make_async_copy(ref, rows_held.at[pl.ds(i * per_member, per_member)], state_sem.at[i])
        )
        loads[-1].start()
    first = 0
    tile_loads = []
    for g, ways in enumerate(tile_ways):
        options = [
            pltpu.make_async_copy(tiles[first + w], lists.at[g], tile_sem.at[g]) for w in range(len(ways))
        ]
        for w, option in enumerate(options):
            if len(options) == 1:
                option.start()
            else:
                pl.when(home[2] == w)(option.start)
        tile_loads.append(options[0])
        first += len(ways)
    weight_loads = []
    done = {}
    for n, ref in enumerate(weights):
        i = n_member(n, n_weights, members)
        start = pl.multiple_of(lax.bitwise_xor(home[0], i) * block, block)
        low = done.get(i, 0)
        done[i] = low + ref.shape[0]
        weight_loads.append(
            pltpu.make_async_copy(
                ref, held.at[pl.ds(low, ref.shape[0]), pl.ds(start, block), :], weight_sem.at[n]
            )
        )
        weight_loads[-1].start()
    for load in loads:
        load.wait()
    for g, j in enumerate(js):
        tile_loads[g].wait()

        def step(n, _, g=g, j=j):
            for u in range(GROUP):
                s = n * GROUP + u
                rows = rows_held[table[0, j * slots + s]]
                made[g, s] = jnp.dot(lists[g, s], rows, preferred_element_type=F32).astype(BF16)
            return 0

        lax.fori_loop(0, counts[j], step, 0)
    for load in weight_loads:
        load.wait()
    for g, j in enumerate(js):
        acc[:per_tile] = jnp.zeros((per_tile,) + acc.shape[1:], F32)

        def step(n, _, g=g, j=j):
            for u in range(GROUP):
                s = n * GROUP + u
                target = table[1, j * slots + s]
                acc[target] += jnp.dot(
                    made[g, s], held[table[2, j * slots + s]], preferred_element_type=F32
                )
            return 0

        lax.fori_loop(0, counts[j], step, 0)
        for r in range(n_rel):
            start = pl.multiple_of(lax.bitwise_xor(home[1], r) * own, own)
            out = outs[g * n_rel + r]
            for t in range(per_tile):
                out[t * tile_rows:(t + 1) * tile_rows] = acc[t, :, pl.ds(start, own)].astype(out.dtype)


def n_member(n, n_weights, members):
    whole = 2 * members - n_weights
    return n if n < whole else whole + (n - whole) // 2


def finish_kernel(state, gate_open, bias, *refs):
    terms, out = refs[:-1], refs[-1]
    message = sum(term[...].astype(F32) for term in terms)
    update = jnp.tanh(message + bias[...])
    opened = gate_open[...]
    out[...] = ((1.0 - opened) * state[...].astype(F32) + opened * update).astype(BF16)


def shards(
    n_rel, n_ent, chunks, state, rel_weight, gate_weight, gate_bias, update_bias,
    tile_values, tile_index, tile_count
):
    members = n_ent // chunks
    rel_dev, _, features = rel_weight.shape
    ent_dev, own_features = state.shape
    tile_rows = tile_values.shape[-1]
    slots = tile_values.shape[1]
    per_tile = ent_dev // tile_rows
    width = features // chunks
    rel = lax.axis_index("rel")
    ent = lax.axis_index("ent")
    part, member = ent // members, ent % members
    line = chunks == 4 and members == 4 and n_rel == 2

    def along(value, pairs):
        perm = [(a * members + m, b * members + m) for a, b in pairs for m in range(members)]
        return lax.ppermute(value, "ent", perm)

    def partner(value, j):
        return along(value, [(q, q ^ j) for q in range(chunks)])

    halves = [state] + [swap(state, "rel", n_rel, r) for r in range(1, n_rel)]

    values = tile_values[0]
    if line:
        near = along(values, [(0, 1), (1, 0), (2, 3), (3, 2)])
        middle = along(values, [(1, 2), (2, 1)])
        inward = along(values, [(0, 2), (3, 1)])
        edge_two = along(middle, [(2, 3), (1, 0)])
        edge_three = along(inward, [(2, 3), (1, 0)])
        tiles = [[values], [near], [inward, edge_two], [middle, edge_three]]
    else:
        tiles = [[values]] + [[partner(values, j)] for j in range(1, chunks)]

    note = jnp.zeros((NOTE_ROWS, width), BF16)
    note = note.at[:3, :slots].set(tile_index[0].astype(BF16))
    note = note.at[3, :1].set(tile_count[0].astype(BF16))
    asked = lax.bitwise_xor(part, jnp.arange(chunks, dtype=jnp.int32))
    per_half = chunks // n_rel
    where = jnp.stack([lax.bitwise_xor(asked // per_half, rel), (asked % per_half) * width])
    pieces = pl.pallas_call(
        functools.partial(pack_kernel, n_rel),
        out_shape=[
            jax.ShapeDtypeStruct((ent_dev + (NOTE_ROWS if j else 0), width), BF16)
            for j in range(chunks)
        ],
        in_specs=[SMEM] + [VMEM] * (n_rel + 1),
        out_specs=[VMEM] * chunks,
        compiler_params=pltpu.CompilerParams(vmem_limit_bytes=8 << 20),
        name="pack",
    )(where, note, *halves)
    moved = [partner(pieces[j], j) for j in range(1, chunks)]
    own = jnp.stack([pieces[0]] + [m[:ent_dev] for m in moved])
    notes = jnp.stack([note] + [m[ent_dev:] for m in moved])
    notes = notes[:, :4, :slots].astype(jnp.int32)
    counts = notes[:, 3, 0]
    source, target, relation = notes[:, 0], notes[:, 1], notes[:, 2]
    live = jnp.arange(slots, dtype=jnp.int32)[None] < counts[:, None]
    owner = source // per_tile
    place = lax.bitwise_xor(owner % members, member) * chunks
    place = (place + lax.bitwise_xor(part, owner // members)) * per_tile + source % per_tile
    table = jnp.stack([
        jnp.where(live, place, 0).reshape(-1),
        jnp.where(live, target, per_tile).reshape(-1),
        jnp.where(live, relation, 0).reshape(-1),
    ])
    turns = (counts + GROUP - 1) // GROUP

    own = own.reshape(chunks * per_tile, tile_rows, width)
    cut = max(1, rel_dev - max(1, rel_dev // 4))
    parts = (rel_weight[:cut], rel_weight[cut:])
    states, weights = [own], [(rel_weight,)]
    high = True
    bits = [1 << b for b in reversed(range(members.bit_length() - 1))]
    order = [0]
    for bit in bits:
        states = states + [swap(v, "ent", n_ent, bit) for v in states]
        more = []
        for i, held in enumerate(weights):
            if i == 0 and high:
                more.append(tuple(swap(v, "ent", n_ent, bit) for v in parts))
            elif i == 0:
                more.append((swap(rel_weight, "ent", n_ent, bit),))
            else:
                more.append(tuple(swap(v, "ent", n_ent, bit) for v in held))
        weights = weights + more
        order = order + [o | bit for o in order]
        high = False
    states = [states[order.index(i)] for i in range(members)]
    weights = [weights[order.index(i)] for i in range(members)]
    whole = [w for w in weights if len(w) == 1]
    assert all(len(w) == 1 for w in weights[:len(whole)])
    weights = [v for held in weights for v in held]
    edge = jnp.logical_or(part == 0, part == chunks - 1).astype(jnp.int32)
    home = jnp.stack([member, rel, edge])

    gate_open = pl.pallas_call(
        functools.partial(gate_kernel, n_rel),
        out_shape=jax.ShapeDtypeStruct((ent_dev, own_features), F32),
        in_specs=[SMEM] + [VMEM] * (n_rel + 2),
        out_specs=VMEM,
        compiler_params=pltpu.CompilerParams(vmem_limit_bytes=12 << 20),
        name="gate",
    )(rel.reshape(1), gate_weight, gate_bias[None], *halves)

    def partial_messages(js):
        ways = [tiles[j] for j in js]
        flat = [t for way in ways for t in way]
        plan = (js, members, tuple((0,) * len(way) for way in ways), len(weights), n_rel, tile_rows)
        n = len(js)
        shapes = []
        for _ in js:
            shapes.append(jax.ShapeDtypeStruct((ent_dev, own_features), F32))
            shapes += [jax.ShapeDtypeStruct((ent_dev, own_features), BF16)] * (n_rel - 1)
        return pl.pallas_call(
            functools.partial(messages_kernel, plan),
            out_shape=shapes,
            in_specs=[SMEM] * 3 + [ANY] * (members + len(flat) + len(weights)),
            out_specs=[VMEM] * len(shapes),
            scratch_shapes=[
                pltpu.VMEM((members * chunks * per_tile, tile_rows, width), BF16),
                pltpu.VMEM((n, slots, tile_rows, tile_rows), BF16),
                pltpu.VMEM((n, slots, tile_rows, width), BF16),
                pltpu.VMEM((rel_dev, width, features), BF16),
                pltpu.VMEM((per_tile + 1, tile_rows, features), F32),
                pltpu.SemaphoreType.DMA((members,)),
                pltpu.SemaphoreType.DMA((n,)),
                pltpu.SemaphoreType.DMA((len(weights),)),
            ],
            cost_estimate=pl.CostEstimate(
                flops=2 * n * slots * tile_rows * width * (features + tile_rows),
                bytes_accessed=2 * rel_dev * width * features,
                transcendentals=0,
            ),
            compiler_params=pltpu.CompilerParams(vmem_limit_bytes=24 << 20),
        )(table, turns, home, *states, *flat, *weights)

    half = chunks // 2
    far = tuple(reversed(range(half, chunks)))
    close = tuple(reversed(range(half)))
    terms = []
    made = list(partial_messages(far)) + list(partial_messages(close))
    for g, j in enumerate(far + close):
        term = made[g * n_rel]
        for r in range(1, n_rel):
            term = term + swap(made[g * n_rel + r], "rel", n_rel, r).astype(F32)
        if j:
            term = partner(term.astype(BF16), j)
        terms.append(term)
    return pl.pallas_call(
        finish_kernel,
        out_shape=jax.ShapeDtypeStruct((ent_dev, own_features), BF16),
        in_specs=[VMEM] * (3 + len(terms)),
        out_specs=VMEM,
        compiler_params=pltpu.CompilerParams(vmem_limit_bytes=12 << 20),
        name="finish",
    )(state, gate_open, update_bias[None], *terms)


def solution(mesh):
    n_rel, n_ent = mesh.shape["rel"], mesh.shape["ent"]
    chunks = max(4, n_rel)
    in_specs = (
        P("ent", "rel"),
        P("rel", "ent", None),
        P(None, "rel"),
        P("rel"),
        P("rel"),
        P("rel", "ent", None, None),
        P("rel", None, "ent"),
        P("rel", "ent"),
    )
    return jax.shard_map(
        functools.partial(shards, n_rel, n_ent, chunks),
        mesh=mesh, in_specs=in_specs, out_specs=P("ent", "rel"), check_vma=False,
    )
```

```python
import functools

import jax
import jax.numpy as jnp
from jax import lax
from jax.experimental import pallas as pl
from jax.experimental.pallas import tpu as pltpu
from jax.sharding import PartitionSpec as P


F32 = jnp.float32
BF16 = jnp.bfloat16
ANY = pl.BlockSpec(memory_space=pl.ANY)
SMEM = pl.BlockSpec(memory_space=pltpu.SMEM)
VMEM = pl.BlockSpec(memory_space=pltpu.VMEM)
GROUP = 4
NOTE_ROWS = 16


def swap(value, axis, size, bit):
    return lax.ppermute(value, axis, [(i, i ^ bit) for i in range(size)])


def pack_kernel(n_rel, where, note, *refs):
    halves, outs = refs[:n_rel], refs[n_rel:]
    rows, width = halves[0].shape[0], outs[0].shape[1]
    for j, out in enumerate(outs):
        start = pl.multiple_of(where[1, j], width)
        for r, half in enumerate(halves):

            @pl.when(where[0, j] == r)
            def _(half=half, out=out, start=start):
                out[:rows] = half[:, pl.ds(start, width)]

        out[rows:] = note[...]


def gate_kernel(n_rel, rel, weight, bias, *refs):
    halves, out = refs[:n_rel], refs[n_rel]
    depth = halves[0].shape[1]
    total = jnp.zeros(out.shape, F32) + bias[...]
    for r, half in enumerate(halves):
        start = pl.multiple_of(lax.bitwise_xor(rel[0], r) * depth, depth)
        total += jnp.dot(half[...], weight[pl.ds(start, depth), :], preferred_element_type=F32)
    out[...] = jax.nn.sigmoid(total)


def stack_kernel(count, *refs):
    pieces, (out, notes) = refs[:count], refs[count:]
    rows = out.shape[1]
    for j, piece in enumerate(pieces):
        out[j] = piece[:rows]
        notes[j] = piece[rows:]


def take(refs, *counts):
    out = []
    for count in counts:
        out.append(refs[:count])
        refs = refs[count:]
    return out + [refs]


def start_tiles(way_counts, way, tiles, lists, sems):
    loads = []
    for g, count in enumerate(way_counts):
        options = [pltpu.make_async_copy(tiles[w], lists.at[g], sems.at[g]) for w in range(count)]
        tiles = tiles[count:]
        for w, option in enumerate(options):
            if count == 1:
                option.start()
            else:
                pl.when(way == w)(option.start)
        loads.append(options[0])
    return loads


def start_weights(members, member, weights, held, sems):
    half = members // 2
    per_block = len(weights) // half
    loads = []
    for n, ref in enumerate(weights):
        i, p = n // per_block, n % per_block
        block = ref.shape[1]
        low = sum(weights[i * per_block + q].shape[0] for q in range(p))
        start = pl.multiple_of(lax.bitwise_xor(i, member % half) * block, block)
        loads.append(
            pltpu.make_async_copy(
                ref, held.at[pl.ds(low, ref.shape[0]), pl.ds(start, block), :], sems.at[n]
            )
        )
        loads[-1].start()
    return loads


def multiply_tiles(turns, table, base, swapped, lists, rows_held, made):
    def step(n, _):
        for u in range(GROUP):
            s = n * GROUP + u
            product = jnp.dot(lists[s], rows_held[table[0, base + s]], preferred_element_type=F32)
            turned = pltpu.roll(product, product.shape[1] // 2, 1)
            made[s] = jnp.where(swapped, turned, product).astype(BF16)
        return 0

    lax.fori_loop(0, turns, step, 0)


def add_messages(turns, table, base, made, own, other, acc):
    acc[:-1] = jnp.zeros((acc.shape[0] - 1,) + acc.shape[1:], F32)

    def step(n, _):
        for u in range(GROUP):
            s = n * GROUP + u
            relation = table[2, base + s]
            weight = jnp.concatenate([own[relation], other[relation]], axis=0)
            acc[table[1, base + s]] += jnp.dot(made[s], weight, preferred_element_type=F32)
        return 0

    lax.fori_loop(0, turns, step, 0)


def put_messages(n_rel, rel, acc, outs):
    per_tile, tile_rows, features = acc.shape[0] - 1, acc.shape[1], acc.shape[2]
    own = features // n_rel
    for r in range(n_rel):
        start = pl.multiple_of(lax.bitwise_xor(rel, r) * own, own)
        for t in range(per_tile):
            outs[r][t * tile_rows:(t + 1) * tile_rows] = acc[t, :, pl.ds(start, own)].astype(outs[r].dtype)


def early_kernel(members, way_counts, n_weights, table, turns, home, *refs):
    states, tiles, weights, rest = take(refs, members, sum(way_counts), n_weights)
    made, held, rows_held, lists, state_sem, tile_sem, weight_sem = rest
    slots = lists.shape[1]
    per_member = states[0].shape[0]
    loads = [
        pltpu.make_async_copy(ref, rows_held.at[pl.ds(i * per_member, per_member)], state_sem.at[i])
        for i, ref in enumerate(states)
    ]
    for load in loads:
        load.start()
    tile_loads = start_tiles(way_counts, home[2], tiles, lists, tile_sem)
    weight_loads = start_weights(members, home[0], weights, held, weight_sem)
    for load in loads:
        load.wait()
    swapped = home[0] >= members // 2
    for j, load in enumerate(tile_loads):
        load.wait()
        multiply_tiles(turns[j], table, j * slots, swapped, lists.at[j], rows_held, made.at[j])
    for load in weight_loads:
        load.wait()


def first_kernel(members, j, n_rel, n_weights, table, turns, home, made, own, *refs):
    weights, outs, rest = take(refs, n_weights, n_rel)
    other, acc, weight_sem = rest
    slots = made.shape[1]
    for load in start_weights(members, home[0], weights, other, weight_sem):
        load.wait()
    add_messages(turns[j], table, j * slots, made.at[j], own, other, acc)
    put_messages(n_rel, home[1], acc, outs)


def late_kernel(members, way_counts, js, n_rel, table, turns, home, rows_held, own, other, *refs):
    tiles, outs, rest = take(refs, sum(way_counts), len(js) * n_rel)
    lists, made, acc, tile_sem = rest
    slots = lists.shape[1]
    loads = start_tiles(way_counts, home[2], tiles, lists, tile_sem)
    for g, j in enumerate(js):
        loads[g].wait()
        multiply_tiles(
            turns[j], table, j * slots, home[0] >= members // 2, lists.at[g], rows_held, made.at[g]
        )
        add_messages(turns[j], table, j * slots, made.at[g], own, other, acc)
        put_messages(n_rel, home[1], acc, outs[g * n_rel:(g + 1) * n_rel])


def near_kernel(js, n_rel, table, turns, home, made, own, other, *refs):
    outs, acc = refs[:-1], refs[-1]
    slots = made.shape[1]
    for g, j in enumerate(js):
        add_messages(turns[j], table, j * slots, made.at[j], own, other, acc)
        put_messages(n_rel, home[1], acc, outs[g * n_rel:(g + 1) * n_rel])


def finish_kernel(used, state, gate_open, bias, *refs):
    terms, out = refs[:-1], refs[-1]
    message = sum(term[...].astype(F32) for term in terms[:-1])
    message = jnp.where(used[0] == 1, message + terms[-1][...].astype(F32), message)
    update = jnp.tanh(message + bias[...])
    opened = gate_open[...]
    out[...] = ((1.0 - opened) * state[...].astype(F32) + opened * update).astype(BF16)


def shards(
    n_rel, n_ent, chunks, state, rel_weight, gate_weight, gate_bias, update_bias,
    tile_values, tile_index, tile_count
):
    members = n_ent // chunks
    rel_dev, _, features = rel_weight.shape
    ent_dev, own_features = state.shape
    tile_rows = tile_values.shape[-1]
    slots = tile_values.shape[1]
    per_tile = ent_dev // tile_rows
    width = features // chunks
    rel = lax.axis_index("rel")
    ent = lax.axis_index("ent")
    part, member = ent // members, ent % members
    line = chunks == 4 and members == 4 and n_rel == 2

    def along(value, pairs):
        perm = [(a * members + m, b * members + m) for a, b in pairs for m in range(members)]
        return lax.ppermute(value, "ent", perm)

    def partner(value, j):
        return along(value, [(q, q ^ j) for q in range(chunks)])

    halves = [state] + [swap(state, "rel", n_rel, r) for r in range(1, n_rel)]

    values = tile_values[0]
    if line:
        near = along(values, [(0, 1), (1, 0), (2, 3), (3, 2)])
        middle = along(values, [(1, 2), (2, 1)])
        inward = along(values, [(0, 2), (3, 1)])
        edge_two = along(middle, [(2, 3), (1, 0)])
        edge_three = along(inward, [(2, 3), (1, 0)])
        tiles = [[values], [near], [inward, edge_two], [middle, edge_three]]
    else:
        tiles = [[values]] + [[partner(values, j)] for j in range(1, chunks)]

    note = jnp.zeros((NOTE_ROWS, width), BF16)
    note = note.at[:3, :slots].set(tile_index[0].astype(BF16))
    note = note.at[3, :1].set(tile_count[0].astype(BF16))
    asked = lax.bitwise_xor(part, jnp.arange(chunks, dtype=jnp.int32))
    per_half = chunks // n_rel
    where = jnp.stack([lax.bitwise_xor(asked // per_half, rel), (asked % per_half) * width])
    pieces = pl.pallas_call(
        functools.partial(pack_kernel, n_rel),
        out_shape=[jax.ShapeDtypeStruct((ent_dev + NOTE_ROWS, width), BF16) for _ in range(chunks)],
        in_specs=[SMEM] + [VMEM] * (n_rel + 1),
        out_specs=[VMEM] * chunks,
        compiler_params=pltpu.CompilerParams(vmem_limit_bytes=8 << 20),
        name="pack",
    )(where, note, *halves)
    moved = [partner(pieces[j], j) for j in range(1, chunks)]
    own, notes = pl.pallas_call(
        functools.partial(stack_kernel, chunks),
        out_shape=[
            jax.ShapeDtypeStruct((chunks, ent_dev, width), BF16),
            jax.ShapeDtypeStruct((chunks, NOTE_ROWS, width), BF16),
        ],
        in_specs=[VMEM] * chunks,
        out_specs=[VMEM] * 2,
        compiler_params=pltpu.CompilerParams(vmem_limit_bytes=8 << 20),
        name="stk",
    )(pieces[0], *moved)
    notes = notes[:, :4, :slots].astype(jnp.int32)
    counts = notes[:, 3, 0]
    source, target, relation = notes[:, 0], notes[:, 1], notes[:, 2]
    live = jnp.arange(slots, dtype=jnp.int32)[None] < counts[:, None]
    owner = source // per_tile
    place = lax.bitwise_xor(owner % members, member) * chunks
    place = (place + lax.bitwise_xor(part, owner // members)) * per_tile + source % per_tile
    table = jnp.stack([
        jnp.where(live, place, 0).reshape(-1),
        jnp.where(live, target, per_tile).reshape(-1),
        jnp.where(live, relation, 0).reshape(-1),
    ])
    turns = (counts + GROUP - 1) // GROUP

    own = own.reshape(chunks * per_tile, tile_rows, width)
    cut = max(1, rel_dev - max(1, rel_dev // 4))
    parts = (rel_weight[:cut], rel_weight[cut:])
    states, weights = [own], [(rel_weight,)]
    high = True
    bits = [1 << b for b in reversed(range(members.bit_length() - 1))]
    order = [0]
    for bit in bits:
        states = states + [swap(v, "ent", n_ent, bit) for v in states]
        more = []
        for i, held in enumerate(weights):
            if i == 0 and high:
                more.append(tuple(swap(v, "ent", n_ent, bit) for v in parts))
            elif i == 0:
                more.append((swap(rel_weight, "ent", n_ent, bit),))
            else:
                more.append(tuple(swap(v, "ent", n_ent, bit) for v in held))
        weights = weights + more
        order = order + [o | bit for o in order]
        high = False
    states = [states[order.index(i)] for i in range(members)]
    weights = [weights[order.index(i)] for i in range(members)]
    own_weights = [v for held in weights[:members // 2] for v in held]
    other_weights = [v for held in weights[members // 2:] for v in held]
    edge = jnp.logical_or(part == 0, part == chunks - 1).astype(jnp.int32)
    home = jnp.stack([member, rel, edge])

    gate_open = pl.pallas_call(
        functools.partial(gate_kernel, n_rel),
        out_shape=jax.ShapeDtypeStruct((ent_dev, own_features), F32),
        in_specs=[SMEM] + [VMEM] * (n_rel + 2),
        out_specs=VMEM,
        compiler_params=pltpu.CompilerParams(vmem_limit_bytes=12 << 20),
        name="gate",
    )(rel.reshape(1), gate_weight, gate_bias[None], *halves)

    early, late = tuple(range(3)), tuple(range(3, chunks))
    early_ways = [len(tiles[j]) for j in early]
    late_ways = [len(tiles[j]) for j in late]
    half_shape = (rel_dev, width // 2, features)
    products = jax.ShapeDtypeStruct((len(early), slots, tile_rows, width), BF16)
    acc_scratch = pltpu.VMEM((per_tile + 1, tile_rows, features), F32)

    def call(body, operands, in_specs, out_shape, scratch, flops):
        return pl.pallas_call(
            body,
            out_shape=out_shape,
            in_specs=[SMEM] * 3 + in_specs,
            out_specs=[VMEM] * len(out_shape),
            scratch_shapes=scratch,
            cost_estimate=pl.CostEstimate(
                flops=flops, bytes_accessed=rel_dev * width * features, transcendentals=0
            ),
            compiler_params=pltpu.CompilerParams(vmem_limit_bytes=16 << 20),
        )(table, turns, home, *operands)

    def message_shapes(count):
        shape = (ent_dev, own_features)
        one = [jax.ShapeDtypeStruct(shape, F32)] + [jax.ShapeDtypeStruct(shape, BF16)] * (n_rel - 1)
        return one * count

    slot_flops = 2 * slots * tile_rows * width
    flat = [t for j in early for t in tiles[j]]
    made, own_half, rows_held = call(
        functools.partial(early_kernel, members, early_ways, len(own_weights)),
        [*states, *flat, *own_weights],
        [ANY] * (members + len(flat) + len(own_weights)),
        [
            products,
            jax.ShapeDtypeStruct(half_shape, BF16),
            jax.ShapeDtypeStruct((members * chunks * per_tile, tile_rows, width), BF16),
        ],
        [
            pltpu.VMEM((len(early), slots, tile_rows, tile_rows), BF16),
            pltpu.SemaphoreType.DMA((members,)),
            pltpu.SemaphoreType.DMA((len(early),)),
            pltpu.SemaphoreType.DMA((len(own_weights),)),
        ],
        len(early) * slot_flops * tile_rows,
    )
    *two, other_half = call(
        functools.partial(first_kernel, members, 2, n_rel, len(other_weights)),
        [made, own_half, *other_weights],
        [VMEM] * 2 + [ANY] * len(other_weights),
        message_shapes(1) + [jax.ShapeDtypeStruct(half_shape, BF16)],
        [acc_scratch, pltpu.SemaphoreType.DMA((len(other_weights),))],
        slot_flops * features,
    )
    flat = [t for j in late for t in tiles[j]]
    rest = call(
        functools.partial(late_kernel, members, late_ways, late, n_rel),
        [rows_held, own_half, other_half, *flat],
        [VMEM] * 3 + [ANY] * len(flat),
        message_shapes(len(late)),
        [
            pltpu.VMEM((len(late), slots, tile_rows, tile_rows), BF16),
            pltpu.VMEM((len(late), slots, tile_rows, width), BF16),
            acc_scratch,
            pltpu.SemaphoreType.DMA((len(late),)),
        ],
        len(late) * slot_flops * (features + tile_rows),
    )
    results = {2: two}
    for j in (1, 0):
        results[j] = call(
            functools.partial(near_kernel, (j,), n_rel),
            [made, own_half, other_half],
            [VMEM] * 3,
            message_shapes(1),
            [acc_scratch],
            slot_flops * features,
        )
    for g, j in enumerate(late):
        results[j] = rest[g * n_rel:(g + 1) * n_rel]

    def summed(j):
        term = results[j][0]
        for r in range(1, n_rel):
            term = term + swap(results[j][r], "rel", n_rel, r).astype(F32)
        return term

    if line:
        passed = along(summed(2).astype(BF16), [(0, 1), (1, 3), (3, 2), (2, 0)])
        three = summed(3)
        across = along(three.astype(BF16), [(0, 3), (3, 0)])
        total = (three + passed.astype(F32)).astype(BF16)
        total = along(total, [(1, 2), (2, 1)])
        terms = [summed(0), partner(summed(1).astype(BF16), 1), across, total, passed]
        used = edge
    else:
        terms = [summed(0)]
        terms += [partner(summed(j).astype(BF16), j) for j in range(1, chunks)]
        used = jnp.ones((), jnp.int32)
    return pl.pallas_call(
        finish_kernel,
        out_shape=jax.ShapeDtypeStruct((ent_dev, own_features), BF16),
        in_specs=[SMEM] + [VMEM] * (3 + len(terms)),
        out_specs=VMEM,
        compiler_params=pltpu.CompilerParams(vmem_limit_bytes=12 << 20),
        name="finish",
    )(used.reshape(1), state, gate_open, update_bias[None], *terms)


def solution(mesh):
    n_rel, n_ent = mesh.shape["rel"], mesh.shape["ent"]
    chunks = max(4, n_rel)
    in_specs = (
        P("ent", "rel"),
        P("rel", "ent", None),
        P(None, "rel"),
        P("rel"),
        P("rel"),
        P("rel", "ent", None, None),
        P("rel", None, "ent"),
        P("rel", "ent"),
    )
    return jax.shard_map(
        functools.partial(shards, n_rel, n_ent, chunks),
        mesh=mesh, in_specs=in_specs, out_specs=P("ent", "rel"), check_vma=False,
    )
```

```python
import functools

import jax
import jax.numpy as jnp
from jax import lax
from jax.experimental import pallas as pl
from jax.experimental.pallas import tpu as pltpu
from jax.sharding import PartitionSpec as P


F32 = jnp.float32
BF16 = jnp.bfloat16
ANY = pl.BlockSpec(memory_space=pl.ANY)
SMEM = pl.BlockSpec(memory_space=pltpu.SMEM)
VMEM = pl.BlockSpec(memory_space=pltpu.VMEM)
GROUP = 4
NOTE_ROWS = 16


def swap(value, axis, size, bit):
    return lax.ppermute(value, axis, [(i, i ^ bit) for i in range(size)])


def pack_kernel(n_rel, where, note, state, *refs):
    others, outs = refs[:n_rel - 1], refs[n_rel - 1:]
    rows, width = outs[0].shape[0] - NOTE_ROWS, outs[0].shape[1]
    first = pl.multiple_of(where[2, 0], rows)
    for j, out in enumerate(outs):
        start = pl.multiple_of(where[1, j], width)
        for r in range(n_rel):

            @pl.when(where[0, j] == r)
            def _(r=r, out=out, start=start):
                if r:
                    out[:rows] = others[r - 1][:, pl.ds(start, width)]
                else:
                    out[:rows] = state[pl.ds(first, rows), pl.ds(start, width)]

        out[rows:] = note[...]


def gate_kernel(n_rel, rel, weight, bias, *refs):
    halves, out = refs[:n_rel], refs[n_rel]
    depth = halves[0].shape[1]
    total = jnp.zeros(out.shape, F32) + bias[...]
    for r, half in enumerate(halves):
        start = pl.multiple_of(lax.bitwise_xor(rel[0], r) * depth, depth)
        total += jnp.dot(half[...], weight[pl.ds(start, depth), :], preferred_element_type=F32)
    out[...] = jax.nn.sigmoid(total)


def stack_kernel(count, *refs):
    pieces, (out, notes) = refs[:count], refs[count:]
    rows = out.shape[1]
    for j, piece in enumerate(pieces):
        out[j] = piece[:rows]
        notes[j] = piece[rows:]


def take(refs, *counts):
    out = []
    for count in counts:
        out.append(refs[:count])
        refs = refs[count:]
    return out + [refs]


def start_tiles(way_counts, way, tiles, lists, sems):
    loads = []
    for g, count in enumerate(way_counts):
        options = [pltpu.make_async_copy(tiles[w], lists.at[g], sems.at[g]) for w in range(count)]
        tiles = tiles[count:]
        for w, option in enumerate(options):
            if count == 1:
                option.start()
            else:
                pl.when(way == w)(option.start)
        loads.append(options[0])
    return loads


def start_weights(members, member, weights, held, sems):
    half = members // 2
    per_block = len(weights) // half
    loads = []
    for n, ref in enumerate(weights):
        i, p = n // per_block, n % per_block
        block = ref.shape[1]
        low = sum(weights[i * per_block + q].shape[0] for q in range(p))
        start = pl.multiple_of(lax.bitwise_xor(i, member % half) * block, block)
        loads.append(
            pltpu.make_async_copy(
                ref, held.at[pl.ds(low, ref.shape[0]), pl.ds(start, block), :], sems.at[n]
            )
        )
        loads[-1].start()
    return loads


def multiply_tiles(turns, table, base, swapped, lists, rows_held, made):
    tile_rows = lists.shape[1]

    def step(n, _):
        for u in range(GROUP):
            s = n * GROUP + u
            first = pl.multiple_of(table[3, base + s], tile_rows)
            rows = rows_held[table[0, base + s], pl.ds(first, tile_rows), :]
            product = jnp.dot(lists[s], rows, preferred_element_type=F32)
            turned = pltpu.roll(product, product.shape[1] // 2, 1)
            made[s] = jnp.where(swapped, turned, product).astype(BF16)
        return 0

    lax.fori_loop(0, turns, step, 0)


def add_messages(turns, table, base, made, own, other, acc):
    acc[:-1] = jnp.zeros((acc.shape[0] - 1,) + acc.shape[1:], F32)

    def step(n, _):
        for u in range(GROUP):
            s = n * GROUP + u
            relation = table[2, base + s]
            weight = jnp.concatenate([own[relation], other[relation]], axis=0)
            acc[table[1, base + s]] += jnp.dot(made[s], weight, preferred_element_type=F32)
        return 0

    lax.fori_loop(0, turns, step, 0)


def put_messages(n_rel, rel, acc, outs):
    per_tile, tile_rows, features = acc.shape[0] - 1, acc.shape[1], acc.shape[2]
    own = features // n_rel
    for r in range(n_rel):
        start = pl.multiple_of(lax.bitwise_xor(rel, r) * own, own)
        for t in range(per_tile):
            outs[r][t * tile_rows:(t + 1) * tile_rows] = acc[t, :, pl.ds(start, own)].astype(outs[r].dtype)


def early_kernel(members, places, way_counts, n_weights, table, turns, home, *refs):
    states, tiles, weights, rest = take(refs, len(places), sum(way_counts), n_weights)
    made, held, rows_held, lists, state_sem, tile_sem, weight_sem = rest
    slots = lists.shape[1]
    chunks, rows = states[0].shape[0], states[0].shape[1]
    loads = []
    for n, ((i, r), ref) in enumerate(zip(places, states)):
        first = pl.multiple_of(lax.bitwise_xor(home[1], r) * rows, rows)
        to = rows_held.at[pl.ds(i * chunks, chunks), pl.ds(first, rows), :]
        loads.append(pltpu.make_async_copy(ref, to, state_sem.at[n]))
        loads[-1].start()
    tile_loads = start_tiles(way_counts, home[2], tiles, lists, tile_sem)
    weight_loads = start_weights(members, home[0], weights, held, weight_sem)
    for load in loads:
        load.wait()
    swapped = home[0] >= members // 2
    for j, load in enumerate(tile_loads):
        load.wait()
        multiply_tiles(turns[j], table, j * slots, swapped, lists.at[j], rows_held, made.at[j])
    for load in weight_loads:
        load.wait()


def first_kernel(members, j, n_rel, n_weights, table, turns, home, made, own, *refs):
    weights, outs, rest = take(refs, n_weights, n_rel)
    other, acc, weight_sem = rest
    slots = made.shape[1]
    for load in start_weights(members, home[0], weights, other, weight_sem):
        load.wait()
    add_messages(turns[j], table, j * slots, made.at[j], own, other, acc)
    put_messages(n_rel, home[1], acc, outs)


def late_kernel(members, way_counts, js, n_rel, table, turns, home, rows_held, own, other, *refs):
    tiles, outs, rest = take(refs, sum(way_counts), len(js) * n_rel)
    lists, made, acc, tile_sem = rest
    slots = lists.shape[1]
    loads = start_tiles(way_counts, home[2], tiles, lists, tile_sem)
    for g, j in enumerate(js):
        loads[g].wait()
        multiply_tiles(
            turns[j], table, j * slots, home[0] >= members // 2, lists.at[g], rows_held, made.at[g]
        )
        add_messages(turns[j], table, j * slots, made.at[g], own, other, acc)
        put_messages(n_rel, home[1], acc, outs[g * n_rel:(g + 1) * n_rel])


def near_kernel(js, n_rel, table, turns, home, made, own, other, *refs):
    outs, acc = refs[:-1], refs[-1]
    slots = made.shape[1]
    for g, j in enumerate(js):
        add_messages(turns[j], table, j * slots, made.at[j], own, other, acc)
        put_messages(n_rel, home[1], acc, outs[g * n_rel:(g + 1) * n_rel])


def finish_kernel(used, state, gate_open, bias, *refs):
    terms, out = refs[:-1], refs[-1]
    message = sum(term[...].astype(F32) for term in terms[:-1])
    message = jnp.where(used[0] == 1, message + terms[-1][...].astype(F32), message)
    update = jnp.tanh(message + bias[...])
    opened = gate_open[...]
    out[...] = ((1.0 - opened) * state[...].astype(F32) + opened * update).astype(BF16)


def shards(
    n_rel, n_ent, chunks, state, rel_weight, gate_weight, gate_bias, update_bias,
    tile_values, tile_index, tile_count
):
    members = n_ent // chunks
    rel_dev, _, features = rel_weight.shape
    ent_dev, own_features = state.shape
    tile_rows = tile_values.shape[-1]
    slots = tile_values.shape[1]
    per_tile = ent_dev // tile_rows
    width = features // chunks
    rel = lax.axis_index("rel")
    ent = lax.axis_index("ent")
    part, member = ent // members, ent % members
    line = chunks == 4 and members == 4 and n_rel == 2

    def along(value, pairs):
        perm = [(a * members + m, b * members + m) for a, b in pairs for m in range(members)]
        return lax.ppermute(value, "ent", perm)

    def partner(value, j):
        return along(value, [(q, q ^ j) for q in range(chunks)])

    rows = ent_dev // n_rel
    others = []
    for r in range(1, n_rel):
        asked_rows = lax.dynamic_slice_in_dim(state, lax.bitwise_xor(rel, r) * rows, rows, 0)
        others.append(swap(asked_rows, "rel", n_rel, r))
    halves = [state] + [swap(state, "rel", n_rel, r) for r in range(1, n_rel)]

    values = tile_values[0]
    if line:
        near = along(values, [(0, 1), (1, 0), (2, 3), (3, 2)])
        middle = along(values, [(1, 2), (2, 1)])
        inward = along(values, [(0, 2), (3, 1)])
        edge_two = along(middle, [(2, 3), (1, 0)])
        edge_three = along(inward, [(2, 3), (1, 0)])
        tiles = [[values], [near], [inward, edge_two], [middle, edge_three]]
    else:
        tiles = [[values]] + [[partner(values, j)] for j in range(1, chunks)]

    note = jnp.zeros((NOTE_ROWS, width), BF16)
    note = note.at[:3, :slots].set(tile_index[0].astype(BF16))
    note = note.at[3, :1].set(tile_count[0].astype(BF16))
    asked = lax.bitwise_xor(part, jnp.arange(chunks, dtype=jnp.int32))
    per_half = chunks // n_rel
    where = jnp.stack([
        lax.bitwise_xor(asked // per_half, rel),
        (asked % per_half) * width,
        jnp.full((chunks,), rel * rows, jnp.int32),
    ])
    pieces = pl.pallas_call(
        functools.partial(pack_kernel, n_rel),
        out_shape=[jax.ShapeDtypeStruct((rows + NOTE_ROWS, width), BF16) for _ in range(chunks)],
        in_specs=[SMEM] + [VMEM] * (n_rel + 1),
        out_specs=[VMEM] * chunks,
        compiler_params=pltpu.CompilerParams(vmem_limit_bytes=8 << 20),
        name="pack",
    )(where, note, state, *others)
    moved = [partner(pieces[j], j) for j in range(1, chunks)]
    own, notes = pl.pallas_call(
        functools.partial(stack_kernel, chunks),
        out_shape=[
            jax.ShapeDtypeStruct((chunks, rows, width), BF16),
            jax.ShapeDtypeStruct((chunks, NOTE_ROWS, width), BF16),
        ],
        in_specs=[VMEM] * chunks,
        out_specs=[VMEM] * 2,
        compiler_params=pltpu.CompilerParams(vmem_limit_bytes=8 << 20),
        name="stk",
    )(pieces[0], *moved)
    notes = notes[:, :4, :slots].astype(jnp.int32)
    counts = notes[:, 3, 0]
    source, target, relation = notes[:, 0], notes[:, 1], notes[:, 2]
    live = jnp.arange(slots, dtype=jnp.int32)[None] < counts[:, None]
    owner = source // per_tile
    place = lax.bitwise_xor(owner % members, member) * chunks
    place = place + lax.bitwise_xor(part, owner // members)
    table = jnp.stack([
        jnp.where(live, place, 0).reshape(-1),
        jnp.where(live, target, per_tile).reshape(-1),
        jnp.where(live, relation, 0).reshape(-1),
        (source % per_tile * tile_rows).reshape(-1),
    ])
    turns = (counts + GROUP - 1) // GROUP

    cut = max(1, rel_dev * 7 // 12)
    parts = (rel_weight[:cut], rel_weight[cut:])
    bits = [1 << b for b in reversed(range(members.bit_length() - 1))]
    rel_bits = [1 << b for b in reversed(range(n_rel.bit_length() - 1))]
    states, places = [own], [(0, 0)]

    def spread(axis, size, bit):
        more = [swap(v, axis, size, bit) for v in states]
        step = (0, bit) if axis == "rel" else (bit, 0)
        places.extend([(i | step[0], r | step[1]) for i, r in places])
        states.extend(more)

    for bit in bits[:-1]:
        spread("ent", n_ent, bit)
    for bit in rel_bits:
        spread("rel", n_rel, bit)
    spread("ent", n_ent, bits[-1])

    weights, order = [(rel_weight,)], [0]
    for bit in bits:
        more = []
        for i, held in enumerate(weights):
            if i == 0 and bit == bits[0]:
                more.append(tuple(swap(v, "ent", n_ent, bit) for v in parts))
            elif i == 0:
                more.append((swap(rel_weight, "ent", n_ent, bit),))
            else:
                more.append(tuple(swap(v, "ent", n_ent, bit) for v in held))
        weights = weights + more
        order = order + [o | bit for o in order]
    weights = [weights[order.index(i)] for i in range(members)]
    own_weights = [v for held in weights[:members // 2] for v in held]
    other_weights = [v for held in weights[members // 2:] for v in held]
    edge = jnp.logical_or(part == 0, part == chunks - 1).astype(jnp.int32)
    home = jnp.stack([member, rel, edge])

    gate_open = pl.pallas_call(
        functools.partial(gate_kernel, n_rel),
        out_shape=jax.ShapeDtypeStruct((ent_dev, own_features), F32),
        in_specs=[SMEM] + [VMEM] * (n_rel + 2),
        out_specs=VMEM,
        compiler_params=pltpu.CompilerParams(vmem_limit_bytes=12 << 20),
        name="gate",
    )(rel.reshape(1), gate_weight, gate_bias[None], *halves)

    early, late = tuple(range(3)), tuple(range(3, chunks))
    early_ways = [len(tiles[j]) for j in early]
    late_ways = [len(tiles[j]) for j in late]
    half_shape = (rel_dev, width // 2, features)
    products = jax.ShapeDtypeStruct((len(early), slots, tile_rows, width), BF16)
    acc_scratch = pltpu.VMEM((per_tile + 1, tile_rows, features), F32)

    def call(body, operands, in_specs, out_shape, scratch, flops):
        return pl.pallas_call(
            body,
            out_shape=out_shape,
            in_specs=[SMEM] * 3 + in_specs,
            out_specs=[VMEM] * len(out_shape),
            scratch_shapes=scratch,
            cost_estimate=pl.CostEstimate(
                flops=flops, bytes_accessed=rel_dev * width * features, transcendentals=0
            ),
            compiler_params=pltpu.CompilerParams(vmem_limit_bytes=16 << 20),
        )(table, turns, home, *operands)

    def message_shapes(count):
        shape = (ent_dev, own_features)
        one = [jax.ShapeDtypeStruct(shape, F32)] + [jax.ShapeDtypeStruct(shape, BF16)] * (n_rel - 1)
        return one * count

    slot_flops = 2 * slots * tile_rows * width
    flat = [t for j in early for t in tiles[j]]
    made, own_half, rows_held = call(
        functools.partial(early_kernel, members, tuple(places), early_ways, len(own_weights)),
        [*states, *flat, *own_weights],
        [ANY] * (len(states) + len(flat) + len(own_weights)),
        [
            products,
            jax.ShapeDtypeStruct(half_shape, BF16),
            jax.ShapeDtypeStruct((members * chunks, ent_dev, width), BF16),
        ],
        [
            pltpu.VMEM((len(early), slots, tile_rows, tile_rows), BF16),
            pltpu.SemaphoreType.DMA((len(states),)),
            pltpu.SemaphoreType.DMA((len(early),)),
            pltpu.SemaphoreType.DMA((len(own_weights),)),
        ],
        len(early) * slot_flops * tile_rows,
    )
    *two, other_half = call(
        functools.partial(first_kernel, members, 2, n_rel, len(other_weights)),
        [made, own_half, *other_weights],
        [VMEM] * 2 + [ANY] * len(other_weights),
        message_shapes(1) + [jax.ShapeDtypeStruct(half_shape, BF16)],
        [acc_scratch, pltpu.SemaphoreType.DMA((len(other_weights),))],
        slot_flops * features,
    )
    flat = [t for j in late for t in tiles[j]]
    rest = call(
        functools.partial(late_kernel, members, late_ways, late, n_rel),
        [rows_held, own_half, other_half, *flat],
        [VMEM] * 3 + [ANY] * len(flat),
        message_shapes(len(late)),
        [
            pltpu.VMEM((len(late), slots, tile_rows, tile_rows), BF16),
            pltpu.VMEM((len(late), slots, tile_rows, width), BF16),
            acc_scratch,
            pltpu.SemaphoreType.DMA((len(late),)),
        ],
        len(late) * slot_flops * (features + tile_rows),
    )
    results = {2: two}
    for j in (1, 0):
        results[j] = call(
            functools.partial(near_kernel, (j,), n_rel),
            [made, own_half, other_half],
            [VMEM] * 3,
            message_shapes(1),
            [acc_scratch],
            slot_flops * features,
        )
    for g, j in enumerate(late):
        results[j] = rest[g * n_rel:(g + 1) * n_rel]

    def summed(j, dtype=BF16):
        moved = [swap(v, "rel", n_rel, r + 1) for r, v in enumerate(results[j][1:])]
        term = results[j][0]
        for other in moved:
            term = term + other.astype(F32)
        return term.astype(dtype)

    if line:
        passed = along(summed(2), [(0, 1), (1, 3), (3, 2), (2, 0)])
        three = lax.optimization_barrier(summed(3))
        across = along(three, [(0, 3), (3, 0)])
        total = (three.astype(F32) + passed.astype(F32)).astype(BF16)
        total = along(total, [(1, 2), (2, 1)])
        terms = [summed(0, F32), partner(summed(1), 1), across, total, passed]
        used = edge
    else:
        terms = [summed(0, F32)]
        terms += [partner(summed(j), j) for j in range(1, chunks)]
        used = jnp.ones((), jnp.int32)
    return pl.pallas_call(
        finish_kernel,
        out_shape=jax.ShapeDtypeStruct((ent_dev, own_features), BF16),
        in_specs=[SMEM] + [VMEM] * (3 + len(terms)),
        out_specs=VMEM,
        compiler_params=pltpu.CompilerParams(vmem_limit_bytes=12 << 20),
        name="finish",
    )(used.reshape(1), state, gate_open, update_bias[None], *terms)


def solution(mesh):
    n_rel, n_ent = mesh.shape["rel"], mesh.shape["ent"]
    chunks = max(4, n_rel)
    in_specs = (
        P("ent", "rel"),
        P("rel", "ent", None),
        P(None, "rel"),
        P("rel"),
        P("rel"),
        P("rel", "ent", None, None),
        P("rel", None, "ent"),
        P("rel", "ent"),
    )
    return jax.shard_map(
        functools.partial(shards, n_rel, n_ent, chunks),
        mesh=mesh, in_specs=in_specs, out_specs=P("ent", "rel"), check_vma=False,
    )
```

```python
import functools

import jax
import jax.numpy as jnp
from jax import lax
from jax.experimental import pallas as pl
from jax.experimental.pallas import tpu as pltpu
from jax.sharding import PartitionSpec as P


F32 = jnp.float32
BF16 = jnp.bfloat16
ANY = pl.BlockSpec(memory_space=pl.ANY)
SMEM = pl.BlockSpec(memory_space=pltpu.SMEM)
VMEM = pl.BlockSpec(memory_space=pltpu.VMEM)
HBM = pl.BlockSpec(memory_space=pltpu.HBM)
GROUP = 4
NOTE_ROWS = 16

HOME = 16


def swap(value, axis, size, bit):
    return lax.ppermute(value, axis, [(i, i ^ bit) for i in range(size)])


def pack_kernel(n_rel, where, note, *refs):
    halves, outs = refs[:n_rel], refs[n_rel:]
    rows, width = outs[0].shape[0] - NOTE_ROWS, outs[0].shape[1]
    first = pl.multiple_of(where[2, 0], rows)
    for j, out in enumerate(outs):
        start = pl.multiple_of(where[1, j], width)
        for r in range(n_rel):

            @pl.when(where[0, j] == r)
            def _(r=r, out=out, start=start):
                out[:rows] = halves[r][pl.ds(first, rows), pl.ds(start, width)]

        out[rows:] = note[...]


def gate_kernel(n_rel, rel, weight, bias, *refs):
    halves, out = refs[:n_rel], refs[n_rel]
    depth = halves[0].shape[1]
    total = jnp.zeros(out.shape, F32) + bias[...]
    for r, half in enumerate(halves):
        start = pl.multiple_of(lax.bitwise_xor(rel[0], r) * depth, depth)
        total += jnp.dot(half[...], weight[pl.ds(start, depth), :], preferred_element_type=F32)
    out[...] = jax.nn.sigmoid(total)


def stack_kernel(count, *refs):
    pieces, (out, notes) = refs[:count], refs[count:]
    rows = out.shape[1]
    for j, piece in enumerate(pieces):
        out[j] = piece[:rows]
        notes[j] = piece[rows:]


def take(refs, *counts):
    out = []
    for count in counts:
        out.append(refs[:count])
        refs = refs[count:]
    return out + [refs]


def start_tiles(way_counts, way, tiles, lists, sems):
    loads = []
    for g, count in enumerate(way_counts):
        options = [pltpu.make_async_copy(tiles[w], lists.at[g], sems.at[g]) for w in range(count)]
        tiles = tiles[count:]
        for w, option in enumerate(options):
            if count == 1:
                option.start()
            else:
                pl.when(way == w)(option.start)
        loads.append(options[0])
    return loads


def start_weights(members, member, weights, held, sems):
    half = members // 2
    per_block = len(weights) // half
    loads = []
    for n, ref in enumerate(weights):
        i, p = n // per_block, n % per_block
        block = ref.shape[1]
        low = sum(weights[i * per_block + q].shape[0] for q in range(p))
        start = pl.multiple_of(lax.bitwise_xor(i, member % half) * block, block)
        loads.append(
            pltpu.make_async_copy(
                ref, held.at[pl.ds(low, ref.shape[0]), pl.ds(start, block), :], sems.at[n]
            )
        )
        loads[-1].start()
    return loads


def multiply_tiles(turns, table, base, swapped, lists, rows_held, made):
    tile_rows = lists.shape[1]

    def step(n, _):
        for u in range(GROUP):
            s = n * GROUP + u
            first = pl.multiple_of(table[3, base + s], tile_rows)
            rows = rows_held[table[0, base + s], pl.ds(first, tile_rows), :]
            product = jnp.dot(lists[s], rows, preferred_element_type=F32)
            turned = pltpu.roll(product, product.shape[1] // 2, 1)
            made[s] = jnp.where(swapped, turned, product).astype(BF16)
        return 0

    lax.fori_loop(0, turns, step, 0)


def add_messages(turns, table, base, made, own, other, acc):
    acc[:-1] = jnp.zeros((acc.shape[0] - 1,) + acc.shape[1:], F32)

    def step(n, _):
        for u in range(GROUP):
            s = n * GROUP + u
            relation = table[2, base + s]
            weight = jnp.concatenate([own[relation], other[relation]], axis=0)
            acc[table[1, base + s]] += jnp.dot(made[s], weight, preferred_element_type=F32)
        return 0

    lax.fori_loop(0, turns, step, 0)


def put_messages(n_rel, rel, acc, outs):
    per_tile, tile_rows, features = acc.shape[0] - 1, acc.shape[1], acc.shape[2]
    own = features // n_rel
    for r in range(n_rel):
        start = pl.multiple_of(lax.bitwise_xor(rel, r) * own, own)
        for t in range(per_tile):
            outs[r][t * tile_rows:(t + 1) * tile_rows] = acc[t, :, pl.ds(start, own)].astype(outs[r].dtype)


def early_kernel(members, places, way_counts, n_weights, table, *refs):
    states, tiles, weights, rest = take(refs, len(places), sum(way_counts), n_weights)
    made, held, rows_held, lists, state_sem, tile_sem, weight_sem = rest
    slots = lists.shape[1]
    chunks, rows = states[0].shape[0], states[0].shape[1]
    loads = []
    for n, ((i, r), ref) in enumerate(zip(places, states)):
        first = pl.multiple_of(lax.bitwise_xor(table[4, HOME + 1], r) * rows, rows)
        to = rows_held.at[pl.ds(i * chunks, chunks), pl.ds(first, rows), :]
        loads.append(pltpu.make_async_copy(ref, to, state_sem.at[n]))
        loads[-1].start()
    tile_loads = start_tiles(way_counts, table[4, HOME + 2], tiles, lists, tile_sem)
    weight_loads = start_weights(members, table[4, HOME], weights, held, weight_sem)
    for load in loads:
        load.wait()
    swapped = table[4, HOME] >= members // 2
    for j, load in enumerate(tile_loads):
        load.wait()
        multiply_tiles(table[4, j], table, j * slots, swapped, lists.at[j], rows_held, made.at[j])
    for load in weight_loads:
        load.wait()


def first_kernel(members, j, n_rel, n_weights, table, made, own, *refs):
    weights, outs, rest = take(refs, n_weights, n_rel)
    other, acc, weight_sem = rest
    slots = made.shape[1]
    for load in start_weights(members, table[4, HOME], weights, other, weight_sem):
        load.wait()
    add_messages(table[4, j], table, j * slots, made.at[j], own, other, acc)
    put_messages(n_rel, table[4, HOME + 1], acc, outs)


def late_kernel(members, way_counts, js, n_rel, table, rows_held, own, other, *refs):
    tiles, outs, rest = take(refs, sum(way_counts), len(js) * n_rel)
    lists, made, acc, tile_sem = rest
    slots = lists.shape[1]
    loads = start_tiles(way_counts, table[4, HOME + 2], tiles, lists, tile_sem)
    for g, j in enumerate(js):
        loads[g].wait()
        multiply_tiles(
            table[4, j], table, j * slots, table[4, HOME] >= members // 2, lists.at[g], rows_held, made.at[g]
        )
        add_messages(table[4, j], table, j * slots, made.at[g], own, other, acc)
        put_messages(n_rel, table[4, HOME + 1], acc, outs[g * n_rel:(g + 1) * n_rel])


def near_kernel(js, n_rel, table, made, own, other, *refs):
    outs, acc = refs[:-1], refs[-1]
    slots = made.shape[1]
    for g, j in enumerate(js):
        add_messages(table[4, j], table, j * slots, made.at[j], own, other, acc)
        put_messages(n_rel, table[4, HOME + 1], acc, outs[g * n_rel:(g + 1) * n_rel])


def finish_kernel(used, state, gate_open, bias, *refs):
    terms, out = refs[:-1], refs[-1]
    message = sum(term[...].astype(F32) for term in terms[:-1])
    message = jnp.where(used[0] == 1, message + terms[-1][...].astype(F32), message)
    update = jnp.tanh(message + bias[...])
    opened = gate_open[...]
    out[...] = ((1.0 - opened) * state[...].astype(F32) + opened * update).astype(BF16)


def shards(
    n_rel, n_ent, chunks, state, rel_weight, gate_weight, gate_bias, update_bias,
    tile_values, tile_index, tile_count
):
    members = n_ent // chunks
    rel_dev, _, features = rel_weight.shape
    ent_dev, own_features = state.shape
    tile_rows = tile_values.shape[-1]
    slots = tile_values.shape[1]
    per_tile = ent_dev // tile_rows
    width = features // chunks
    rel = lax.axis_index("rel")
    ent = lax.axis_index("ent")
    part, member = ent // members, ent % members
    line = chunks == 4 and members == 4 and n_rel == 2

    def along(value, pairs):
        perm = [(a * members + m, b * members + m) for a, b in pairs for m in range(members)]
        return lax.ppermute(value, "ent", perm)

    def partner(value, j):
        return along(value, [(q, q ^ j) for q in range(chunks)])

    rows = ent_dev // n_rel
    halves = [state] + [swap(state, "rel", n_rel, r) for r in range(1, n_rel)]

    values = tile_values[0]
    if line:
        near = along(values, [(0, 1), (1, 0), (2, 3), (3, 2)])
        middle = along(values, [(1, 2), (2, 1)])
        inward = along(values, [(0, 2), (3, 1)])
        edge_two = along(middle, [(2, 3), (1, 0)])
        edge_three = along(inward, [(2, 3), (1, 0)])
        tiles = [[values], [near], [inward, edge_two], [middle, edge_three]]
    else:
        tiles = [[values]] + [[partner(values, j)] for j in range(1, chunks)]

    note = jnp.zeros((NOTE_ROWS, width), BF16)
    note = note.at[:3, :slots].set(tile_index[0].astype(BF16))
    note = note.at[3, :1].set(tile_count[0].astype(BF16))
    asked = lax.bitwise_xor(part, jnp.arange(chunks, dtype=jnp.int32))
    per_half = chunks // n_rel
    where = jnp.stack([
        lax.bitwise_xor(asked // per_half, rel),
        (asked % per_half) * width,
        jnp.full((chunks,), rel * rows, jnp.int32),
    ])
    pieces = pl.pallas_call(
        functools.partial(pack_kernel, n_rel),
        out_shape=[jax.ShapeDtypeStruct((rows + NOTE_ROWS, width), BF16) for _ in range(chunks)],
        in_specs=[SMEM] + [VMEM] * (n_rel + 1),
        out_specs=[VMEM] * chunks,
        compiler_params=pltpu.CompilerParams(vmem_limit_bytes=8 << 20),
        name="pack",
    )(where, note, *halves)
    moved = [partner(pieces[j], j) for j in range(1, chunks)]
    own, notes = pl.pallas_call(
        functools.partial(stack_kernel, chunks),
        out_shape=[
            jax.ShapeDtypeStruct((chunks, rows, width), BF16),
            jax.ShapeDtypeStruct((chunks, NOTE_ROWS, width), BF16),
        ],
        in_specs=[VMEM] * chunks,
        out_specs=[VMEM] * 2,
        compiler_params=pltpu.CompilerParams(vmem_limit_bytes=8 << 20),
        name="stk",
    )(pieces[0], *moved)
    notes = notes[:, :4, :slots].astype(jnp.int32)
    counts = notes[:, 3, 0]
    source, target, relation = notes[:, 0], notes[:, 1], notes[:, 2]
    live = jnp.arange(slots, dtype=jnp.int32)[None] < counts[:, None]
    owner = source // per_tile
    place = lax.bitwise_xor(owner % members, member) * chunks
    place = place + lax.bitwise_xor(part, owner // members)
    edge = jnp.logical_or(part == 0, part == chunks - 1).astype(jnp.int32)
    turns = (counts + GROUP - 1) // GROUP
    last = jnp.zeros((chunks * slots,), jnp.int32).at[:chunks].set(turns)
    last = last.at[HOME:HOME + 3].set(jnp.stack([member, rel, edge]))
    table = jnp.stack([
        jnp.where(live, place, 0).reshape(-1),
        jnp.where(live, target, per_tile).reshape(-1),
        jnp.where(live, relation, 0).reshape(-1),
        (source % per_tile * tile_rows).reshape(-1),
        last,
    ])

    cut = max(1, rel_dev * 2 // 3)
    parts = (rel_weight[:cut], rel_weight[cut:])
    bits = [1 << b for b in reversed(range(members.bit_length() - 1))]
    rel_bits = [1 << b for b in reversed(range(n_rel.bit_length() - 1))]
    states, places = [own], [(0, 0)]

    def spread(axis, size, bit):
        more = [swap(v, axis, size, bit) for v in states]
        step = (0, bit) if axis == "rel" else (bit, 0)
        places.extend([(i | step[0], r | step[1]) for i, r in places])
        states.extend(more)

    for bit in bits[:-1]:
        spread("ent", n_ent, bit)
    for bit in rel_bits:
        spread("rel", n_rel, bit)
    spread("ent", n_ent, bits[-1])

    weights, order = [(rel_weight,)], [0]
    for bit in bits:
        more = []
        for i, held in enumerate(weights):
            if i == 0 and bit == bits[0]:
                more.append(tuple(swap(v, "ent", n_ent, bit) for v in parts))
            elif i == 0:
                more.append((swap(rel_weight, "ent", n_ent, bit),))
            else:
                more.append(tuple(swap(v, "ent", n_ent, bit) for v in held))
        weights = weights + more
        order = order + [o | bit for o in order]
    weights = [weights[order.index(i)] for i in range(members)]
    own_weights = [v for held in weights[:members // 2] for v in held]
    other_weights = [v for held in weights[members // 2:] for v in held]

    gate_open = pl.pallas_call(
        functools.partial(gate_kernel, n_rel),
        out_shape=jax.ShapeDtypeStruct((ent_dev, own_features), F32),
        in_specs=[SMEM] + [VMEM] * (n_rel + 2),
        out_specs=VMEM,
        compiler_params=pltpu.CompilerParams(vmem_limit_bytes=12 << 20),
        name="gate",
    )(rel.reshape(1), gate_weight, gate_bias[None], *halves)

    early, late = tuple(range(3)), tuple(range(3, chunks))
    early_ways = [len(tiles[j]) for j in early]
    late_ways = [len(tiles[j]) for j in late]
    half_shape = (rel_dev, width // 2, features)
    products = jax.ShapeDtypeStruct((len(early), slots, tile_rows, width), BF16)
    acc_scratch = pltpu.VMEM((per_tile + 1, tile_rows, features), F32)

    def call(body, operands, in_specs, out_shape, scratch, flops):
        return pl.pallas_call(
            body,
            out_shape=out_shape,
            in_specs=[SMEM] + in_specs,
            out_specs=[VMEM] * len(out_shape),
            scratch_shapes=scratch,
            cost_estimate=pl.CostEstimate(
                flops=flops, bytes_accessed=rel_dev * width * features, transcendentals=0
            ),
            compiler_params=pltpu.CompilerParams(vmem_limit_bytes=16 << 20),
        )(table, *operands)

    def message_shapes(count):
        shape = (ent_dev, own_features)
        one = [jax.ShapeDtypeStruct(shape, F32)] + [jax.ShapeDtypeStruct(shape, BF16)] * (n_rel - 1)
        return one * count

    slot_flops = 2 * slots * tile_rows * width
    flat = [t for j in early for t in tiles[j]]
    made, own_half, rows_held = call(
        functools.partial(early_kernel, members, tuple(places), early_ways, len(own_weights)),
        [*states, *flat, *own_weights],
        [HBM if v is values or v is rel_weight else ANY for v in [*states, *flat, *own_weights]],
        [
            products,
            jax.ShapeDtypeStruct(half_shape, BF16),
            jax.ShapeDtypeStruct((members * chunks, ent_dev, width), BF16),
        ],
        [
            pltpu.VMEM((len(early), slots, tile_rows, tile_rows), BF16),
            pltpu.SemaphoreType.DMA((len(states),)),
            pltpu.SemaphoreType.DMA((len(early),)),
            pltpu.SemaphoreType.DMA((len(own_weights),)),
        ],
        len(early) * slot_flops * tile_rows,
    )
    *two, other_half = call(
        functools.partial(first_kernel, members, 2, n_rel, len(other_weights)),
        [made, own_half, *other_weights],
        [VMEM] * 2 + [ANY] * len(other_weights),
        message_shapes(1) + [jax.ShapeDtypeStruct(half_shape, BF16)],
        [acc_scratch, pltpu.SemaphoreType.DMA((len(other_weights),))],
        slot_flops * features,
    )
    flat = [t for j in late for t in tiles[j]]
    rest = call(
        functools.partial(late_kernel, members, late_ways, late, n_rel),
        [rows_held, own_half, other_half, *flat],
        [VMEM] * 3 + [ANY] * len(flat),
        message_shapes(len(late)),
        [
            pltpu.VMEM((len(late), slots, tile_rows, tile_rows), BF16),
            pltpu.VMEM((len(late), slots, tile_rows, width), BF16),
            acc_scratch,
            pltpu.SemaphoreType.DMA((len(late),)),
        ],
        len(late) * slot_flops * (features + tile_rows),
    )
    results = {2: two}
    for j in (1, 0):
        results[j] = call(
            functools.partial(near_kernel, (j,), n_rel),
            [made, own_half, other_half],
            [VMEM] * 3,
            message_shapes(1),
            [acc_scratch],
            slot_flops * features,
        )
    for g, j in enumerate(late):
        results[j] = rest[g * n_rel:(g + 1) * n_rel]

    def summed(j, dtype=BF16):
        moved = [swap(v, "rel", n_rel, r + 1) for r, v in enumerate(results[j][1:])]
        term = results[j][0]
        for other in moved:
            term = term + other.astype(F32)
        return term.astype(dtype)

    if line:
        passed = along(summed(2), [(0, 1), (1, 3), (3, 2), (2, 0)])
        three = lax.optimization_barrier(summed(3))
        across = along(three, [(0, 3), (3, 0)])
        total = (three.astype(F32) + passed.astype(F32)).astype(BF16)
        total = along(total, [(1, 2), (2, 1)])
        terms = [summed(0, F32), partner(summed(1), 1), across, total, passed]
        used = edge
    else:
        terms = [summed(0, F32)]
        terms += [partner(summed(j), j) for j in range(1, chunks)]
        used = jnp.ones((), jnp.int32)
    return pl.pallas_call(
        finish_kernel,
        out_shape=jax.ShapeDtypeStruct((ent_dev, own_features), BF16),
        in_specs=[SMEM] + [VMEM] * (3 + len(terms)),
        out_specs=VMEM,
        compiler_params=pltpu.CompilerParams(vmem_limit_bytes=12 << 20),
        name="finish",
    )(used.reshape(1), state, gate_open, update_bias[None], *terms)


def solution(mesh):
    n_rel, n_ent = mesh.shape["rel"], mesh.shape["ent"]
    chunks = max(4, n_rel)
    in_specs = (
        P("ent", "rel"),
        P("rel", "ent", None),
        P(None, "rel"),
        P("rel"),
        P("rel"),
        P("rel", "ent", None, None),
        P("rel", None, "ent"),
        P("rel", "ent"),
    )
    return jax.shard_map(
        functools.partial(shards, n_rel, n_ent, chunks),
        mesh=mesh, in_specs=in_specs, out_specs=P("ent", "rel"), check_vma=False,
    )
```

```python
import functools

import jax
import jax.numpy as jnp
from jax import lax
from jax.experimental import pallas as pl
from jax.experimental.pallas import tpu as pltpu
from jax.sharding import PartitionSpec as P


F32 = jnp.float32
BF16 = jnp.bfloat16
ANY = pl.BlockSpec(memory_space=pl.ANY)
SMEM = pl.BlockSpec(memory_space=pltpu.SMEM)
VMEM = pl.BlockSpec(memory_space=pltpu.VMEM)
HBM = pl.BlockSpec(memory_space=pltpu.HBM)
GROUP = 4
NOTE_ROWS = 16

HOME = 16


def swap(value, axis, size, bit):
    return lax.ppermute(value, axis, [(i, i ^ bit) for i in range(size)])


def pack_kernel(n_rel, where, note, *refs):
    halves, outs = refs[:n_rel], refs[n_rel:]
    rows, width = outs[0].shape[0] - NOTE_ROWS, outs[0].shape[1]
    first = pl.multiple_of(where[2, 0], rows)
    for j, out in enumerate(outs):
        start = pl.multiple_of(where[1, j], width)
        for r in range(n_rel):

            @pl.when(where[0, j] == r)
            def _(r=r, out=out, start=start):
                out[:rows] = halves[r][pl.ds(first, rows), pl.ds(start, width)]

        out[rows:] = note[...]


def gate_kernel(n_rel, rel, weight, bias, *refs):
    halves, out = refs[:n_rel], refs[n_rel]
    depth = halves[0].shape[1]
    total = jnp.zeros(out.shape, F32) + bias[...]
    for r, half in enumerate(halves):
        start = pl.multiple_of(lax.bitwise_xor(rel[0], r) * depth, depth)
        total += jnp.dot(half[...], weight[pl.ds(start, depth), :], preferred_element_type=F32)
    out[...] = jax.nn.sigmoid(total)


def stack_kernel(count, *refs):
    pieces, (out, notes) = refs[:count], refs[count:]
    rows = out.shape[1]
    for j, piece in enumerate(pieces):
        out[j] = piece[:rows]
        notes[j] = piece[rows:]


def take(refs, *counts):
    out = []
    for count in counts:
        out.append(refs[:count])
        refs = refs[count:]
    return out + [refs]


def start_tiles(way_counts, way, tiles, lists, sems):
    loads = []
    for g, count in enumerate(way_counts):
        options = [pltpu.make_async_copy(tiles[w], lists.at[g], sems.at[g]) for w in range(count)]
        tiles = tiles[count:]
        for w, option in enumerate(options):
            if count == 1:
                option.start()
            else:
                pl.when(way == w)(option.start)
        loads.append(options[0])
    return loads


def start_weights(members, member, weights, held, sems):
    half = members // 2
    per_block = len(weights) // half
    loads = []
    for n, ref in enumerate(weights):
        i, p = n // per_block, n % per_block
        block = ref.shape[1]
        low = sum(weights[i * per_block + q].shape[0] for q in range(p))
        start = pl.multiple_of(lax.bitwise_xor(i, member % half) * block, block)
        loads.append(
            pltpu.make_async_copy(
                ref, held.at[pl.ds(low, ref.shape[0]), pl.ds(start, block), :], sems.at[n]
            )
        )
        loads[-1].start()
    return loads


def multiply_tiles(turns, table, base, swapped, lists, rows_held, made):
    tile_rows = lists.shape[1]

    def step(n, _):
        for u in range(GROUP):
            s = n * GROUP + u
            first = pl.multiple_of(table[3, base + s], tile_rows)
            rows = rows_held[table[0, base + s], pl.ds(first, tile_rows), :]
            product = jnp.dot(lists[s], rows, preferred_element_type=F32)
            turned = pltpu.roll(product, product.shape[1] // 2, 1)
            made[s] = jnp.where(swapped, turned, product).astype(BF16)
        return 0

    lax.fori_loop(0, turns, step, 0)


def add_messages(turns, table, base, made, own, other, acc):
    acc[:-1] = jnp.zeros((acc.shape[0] - 1,) + acc.shape[1:], F32)

    def step(n, _):
        for u in range(GROUP):
            s = n * GROUP + u
            relation = table[2, base + s]
            weight = jnp.concatenate([own[relation], other[relation]], axis=0)
            acc[table[1, base + s]] += jnp.dot(made[s], weight, preferred_element_type=F32)
        return 0

    lax.fori_loop(0, turns, step, 0)


def put_messages(n_rel, rel, acc, outs):
    per_tile, tile_rows, features = acc.shape[0] - 1, acc.shape[1], acc.shape[2]
    own = features // n_rel
    for r in range(n_rel):
        start = pl.multiple_of(lax.bitwise_xor(rel, r) * own, own)
        for t in range(per_tile):
            outs[r][t * tile_rows:(t + 1) * tile_rows] = acc[t, :, pl.ds(start, own)].astype(outs[r].dtype)


def early_kernel(members, places, way_counts, n_weights, table, *refs):
    states, tiles, weights, rest = take(refs, len(places), sum(way_counts), n_weights)
    made, held, rows_held, lists, state_sem, tile_sem, weight_sem = rest
    slots = lists.shape[1]
    chunks, rows = states[0].shape[0], states[0].shape[1]
    loads = []
    for n, ((i, r), ref) in enumerate(zip(places, states)):
        first = pl.multiple_of(lax.bitwise_xor(table[4, HOME + 1], r) * rows, rows)
        to = rows_held.at[pl.ds(i * chunks, chunks), pl.ds(first, rows), :]
        loads.append(pltpu.make_async_copy(ref, to, state_sem.at[n]))
        loads[-1].start()
    tile_loads = start_tiles(way_counts, table[4, HOME + 2], tiles, lists, tile_sem)
    weight_loads = start_weights(members, table[4, HOME], weights, held, weight_sem)
    for load in loads:
        load.wait()
    swapped = table[4, HOME] >= members // 2
    for j, load in enumerate(tile_loads):
        load.wait()
        multiply_tiles(table[4, j], table, j * slots, swapped, lists.at[j], rows_held, made.at[j])
    for load in weight_loads:
        load.wait()


def first_kernel(members, j, n_rel, n_weights, table, made, own, *refs):
    weights, outs, rest = take(refs, n_weights, n_rel)
    other, acc, weight_sem = rest
    slots = made.shape[1]
    for load in start_weights(members, table[4, HOME], weights, other, weight_sem):
        load.wait()
    add_messages(table[4, j], table, j * slots, made.at[j], own, other, acc)
    put_messages(n_rel, table[4, HOME + 1], acc, outs)


def late_kernel(members, way_counts, js, n_rel, table, rows_held, own, other, *refs):
    tiles, outs, rest = take(refs, sum(way_counts), len(js) * n_rel)
    lists, made, acc, tile_sem = rest
    slots = lists.shape[1]
    loads = start_tiles(way_counts, table[4, HOME + 2], tiles, lists, tile_sem)
    for g, j in enumerate(js):
        loads[g].wait()
        multiply_tiles(
            table[4, j], table, j * slots, table[4, HOME] >= members // 2, lists.at[g], rows_held, made.at[g]
        )
        add_messages(table[4, j], table, j * slots, made.at[g], own, other, acc)
        put_messages(n_rel, table[4, HOME + 1], acc, outs[g * n_rel:(g + 1) * n_rel])


def near_kernel(js, n_rel, table, made, own, other, *refs):
    outs, acc = refs[:-1], refs[-1]
    slots = made.shape[1]
    for g, j in enumerate(js):
        add_messages(table[4, j], table, j * slots, made.at[j], own, other, acc)
        put_messages(n_rel, table[4, HOME + 1], acc, outs[g * n_rel:(g + 1) * n_rel])


def finish_kernel(used, state, gate_open, bias, *refs):
    terms, out = refs[:-1], refs[-1]
    message = sum(term[...].astype(F32) for term in terms[:-1])
    message = jnp.where(used[0] == 1, message + terms[-1][...].astype(F32), message)
    update = jnp.tanh(message + bias[...])
    opened = gate_open[...]
    out[...] = ((1.0 - opened) * state[...].astype(F32) + opened * update).astype(BF16)


def shards(
    n_rel, n_ent, chunks, state, rel_weight, gate_weight, gate_bias, update_bias,
    tile_values, tile_index, tile_count
):
    members = n_ent // chunks
    rel_dev, _, features = rel_weight.shape
    ent_dev, own_features = state.shape
    tile_rows = tile_values.shape[-1]
    slots = tile_values.shape[1]
    per_tile = ent_dev // tile_rows
    width = features // chunks
    rel = lax.axis_index("rel")
    ent = lax.axis_index("ent")
    part, member = ent // members, ent % members
    edge = jnp.logical_or(part == 0, part == chunks - 1).astype(jnp.int32)
    line = chunks == 4 and members == 4 and n_rel == 2

    def along(value, pairs):
        perm = [(a * members + m, b * members + m) for a, b in pairs for m in range(members)]
        return lax.ppermute(value, "ent", perm)

    def partner(value, j):
        return along(value, [(q, q ^ j) for q in range(chunks)])

    rows = ent_dev // n_rel
    halves = [state] + [swap(state, "rel", n_rel, r) for r in range(1, n_rel)]

    values = tile_values[0]
    if line:
        near = along(values, [(0, 1), (1, 0), (2, 3), (3, 2)])
        middle = along(values, [(1, 2), (2, 1)])
        onward = jnp.where(edge == 1, values, middle)
        two = along(onward, [(0, 2), (2, 3), (3, 1), (1, 0)])
        edge_three = along(two, [(2, 3), (1, 0)])
        tiles = [[values], [near], [two], [middle, edge_three]]
    else:
        tiles = [[values]] + [[partner(values, j)] for j in range(1, chunks)]

    note = jnp.zeros((NOTE_ROWS, width), BF16)
    note = note.at[:3, :slots].set(tile_index[0].astype(BF16))
    note = note.at[3, :1].set(tile_count[0].astype(BF16))
    asked = lax.bitwise_xor(part, jnp.arange(chunks, dtype=jnp.int32))
    per_half = chunks // n_rel
    where = jnp.stack([
        lax.bitwise_xor(asked // per_half, rel),
        (asked % per_half) * width,
        jnp.full((chunks,), rel * rows, jnp.int32),
    ])
    pieces = pl.pallas_call(
        functools.partial(pack_kernel, n_rel),
        out_shape=[jax.ShapeDtypeStruct((rows + NOTE_ROWS, width), BF16) for _ in range(chunks)],
        in_specs=[SMEM] + [VMEM] * (n_rel + 1),
        out_specs=[VMEM] * chunks,
        compiler_params=pltpu.CompilerParams(vmem_limit_bytes=8 << 20),
        name="pack",
    )(where, note, *halves)
    moved = [partner(pieces[j], j) for j in range(1, chunks)]
    own, notes = pl.pallas_call(
        functools.partial(stack_kernel, chunks),
        out_shape=[
            jax.ShapeDtypeStruct((chunks, rows, width), BF16),
            jax.ShapeDtypeStruct((chunks, NOTE_ROWS, width), BF16),
        ],
        in_specs=[VMEM] * chunks,
        out_specs=[VMEM] * 2,
        compiler_params=pltpu.CompilerParams(vmem_limit_bytes=8 << 20),
        name="stk",
    )(pieces[0], *moved)
    notes = notes[:, :4, :slots].astype(jnp.int32)
    counts = notes[:, 3, 0]
    source, target, relation = notes[:, 0], notes[:, 1], notes[:, 2]
    live = jnp.arange(slots, dtype=jnp.int32)[None] < counts[:, None]
    owner = source // per_tile
    place = lax.bitwise_xor(owner % members, member) * chunks
    place = place + lax.bitwise_xor(part, owner // members)
    turns = (counts + GROUP - 1) // GROUP
    last = jnp.zeros((chunks * slots,), jnp.int32).at[:chunks].set(turns)
    last = last.at[HOME:HOME + 3].set(jnp.stack([member, rel, edge]))
    table = jnp.stack([
        jnp.where(live, place, 0).reshape(-1),
        jnp.where(live, target, per_tile).reshape(-1),
        jnp.where(live, relation, 0).reshape(-1),
        (source % per_tile * tile_rows).reshape(-1),
        last,
    ])

    cut = max(1, rel_dev * 7 // 12)
    parts = (rel_weight[:cut], rel_weight[cut:])
    bits = [1 << b for b in reversed(range(members.bit_length() - 1))]
    rel_bits = [1 << b for b in reversed(range(n_rel.bit_length() - 1))]
    states, places = [own], [(0, 0)]

    def spread(axis, size, bit):
        more = [swap(v, axis, size, bit) for v in states]
        step = (0, bit) if axis == "rel" else (bit, 0)
        places.extend([(i | step[0], r | step[1]) for i, r in places])
        states.extend(more)

    for bit in bits[:-1]:
        spread("ent", n_ent, bit)
    for bit in rel_bits:
        spread("rel", n_rel, bit)
    spread("ent", n_ent, bits[-1])

    weights, order = [(rel_weight,)], [0]
    for bit in bits:
        more = []
        for i, held in enumerate(weights):
            if i == 0 and bit == bits[0]:
                more.append(tuple(swap(v, "ent", n_ent, bit) for v in parts))
            elif i == 0:
                more.append((swap(rel_weight, "ent", n_ent, bit),))
            else:
                more.append(tuple(swap(v, "ent", n_ent, bit) for v in held))
        weights = weights + more
        order = order + [o | bit for o in order]
    weights = [weights[order.index(i)] for i in range(members)]
    own_weights = [v for held in weights[:members // 2] for v in held]
    other_weights = [v for held in weights[members // 2:] for v in held]

    gate_open = pl.pallas_call(
        functools.partial(gate_kernel, n_rel),
        out_shape=jax.ShapeDtypeStruct((ent_dev, own_features), F32),
        in_specs=[SMEM] + [VMEM] * (n_rel + 2),
        out_specs=VMEM,
        compiler_params=pltpu.CompilerParams(vmem_limit_bytes=12 << 20),
        name="gate",
    )(rel.reshape(1), gate_weight, gate_bias[None], *halves)

    early, late = tuple(range(3)), tuple(range(3, chunks))
    early_ways = [len(tiles[j]) for j in early]
    late_ways = [len(tiles[j]) for j in late]
    half_shape = (rel_dev, width // 2, features)
    products = jax.ShapeDtypeStruct((len(early), slots, tile_rows, width), BF16)
    acc_scratch = pltpu.VMEM((per_tile + 1, tile_rows, features), F32)

    def call(body, operands, in_specs, out_shape, scratch, flops):
        return pl.pallas_call(
            body,
            out_shape=out_shape,
            in_specs=[SMEM] + in_specs,
            out_specs=[VMEM] * len(out_shape),
            scratch_shapes=scratch,
            cost_estimate=pl.CostEstimate(
                flops=flops, bytes_accessed=rel_dev * width * features, transcendentals=0
            ),
            compiler_params=pltpu.CompilerParams(vmem_limit_bytes=16 << 20),
        )(table, *operands)

    def message_shapes(count):
        shape = (ent_dev, own_features)
        one = [jax.ShapeDtypeStruct(shape, F32)] + [jax.ShapeDtypeStruct(shape, BF16)] * (n_rel - 1)
        return one * count

    slot_flops = 2 * slots * tile_rows * width
    flat = [t for j in early for t in tiles[j]]
    made, own_half, rows_held = call(
        functools.partial(early_kernel, members, tuple(places), early_ways, len(own_weights)),
        [*states, *flat, *own_weights],
        [HBM if v is values or v is rel_weight else ANY for v in [*states, *flat, *own_weights]],
        [
            products,
            jax.ShapeDtypeStruct(half_shape, BF16),
            jax.ShapeDtypeStruct((members * chunks, ent_dev, width), BF16),
        ],
        [
            pltpu.VMEM((len(early), slots, tile_rows, tile_rows), BF16),
            pltpu.SemaphoreType.DMA((len(states),)),
            pltpu.SemaphoreType.DMA((len(early),)),
            pltpu.SemaphoreType.DMA((len(own_weights),)),
        ],
        len(early) * slot_flops * tile_rows,
    )
    *two, other_half = call(
        functools.partial(first_kernel, members, 2, n_rel, len(other_weights)),
        [made, own_half, *other_weights],
        [VMEM] * 2 + [ANY] * len(other_weights),
        message_shapes(1) + [jax.ShapeDtypeStruct(half_shape, BF16)],
        [acc_scratch, pltpu.SemaphoreType.DMA((len(other_weights),))],
        slot_flops * features,
    )
    results = {2: two}
    for j in (1, 0):
        results[j] = call(
            functools.partial(near_kernel, (j,), n_rel),
            [made, own_half, other_half],
            [VMEM] * 3,
            message_shapes(1),
            [acc_scratch],
            slot_flops * features,
        )
    flat = [t for j in late for t in tiles[j]]
    rest = call(
        functools.partial(late_kernel, members, late_ways, late, n_rel),
        [rows_held, own_half, other_half, *flat],
        [VMEM] * 3 + [ANY] * len(flat),
        message_shapes(len(late)),
        [
            pltpu.VMEM((len(late), slots, tile_rows, tile_rows), BF16),
            pltpu.VMEM((len(late), slots, tile_rows, width), BF16),
            acc_scratch,
            pltpu.SemaphoreType.DMA((len(late),)),
        ],
        len(late) * slot_flops * (features + tile_rows),
    )
    for g, j in enumerate(late):
        results[j] = rest[g * n_rel:(g + 1) * n_rel]

    def summed(j, dtype=BF16):
        moved = [swap(v, "rel", n_rel, r + 1) for r, v in enumerate(results[j][1:])]
        term = results[j][0]
        for other in moved:
            term = term + other.astype(F32)
        return term.astype(dtype)

    if line:
        passed = along(summed(2), [(0, 1), (1, 3), (3, 2), (2, 0)])
        three = lax.optimization_barrier(summed(3))
        across = along(three, [(0, 3), (3, 0)])
        total = (three.astype(F32) + passed.astype(F32)).astype(BF16)
        total = along(total, [(1, 2), (2, 1)])
        terms = [summed(0, F32), partner(summed(1), 1), across, total, passed]
        used = edge
    else:
        terms = [summed(0, F32)]
        terms += [partner(summed(j), j) for j in range(1, chunks)]
        used = jnp.ones((), jnp.int32)
    return pl.pallas_call(
        finish_kernel,
        out_shape=jax.ShapeDtypeStruct((ent_dev, own_features), BF16),
        in_specs=[SMEM] + [VMEM] * (3 + len(terms)),
        out_specs=VMEM,
        compiler_params=pltpu.CompilerParams(vmem_limit_bytes=12 << 20),
        name="finish",
    )(used.reshape(1), state, gate_open, update_bias[None], *terms)


def solution(mesh):
    n_rel, n_ent = mesh.shape["rel"], mesh.shape["ent"]
    chunks = max(4, n_rel)
    in_specs = (
        P("ent", "rel"),
        P("rel", "ent", None),
        P(None, "rel"),
        P("rel"),
        P("rel"),
        P("rel", "ent", None, None),
        P("rel", None, "ent"),
        P("rel", "ent"),
    )
    return jax.shard_map(
        functools.partial(shards, n_rel, n_ent, chunks),
        mesh=mesh, in_specs=in_specs, out_specs=P("ent", "rel"), check_vma=False,
    )
```

```python
import functools

import jax
import jax.numpy as jnp
from jax import lax
from jax.experimental import pallas as pl
from jax.experimental.pallas import tpu as pltpu
from jax.sharding import PartitionSpec as P


F32 = jnp.float32
BF16 = jnp.bfloat16
ANY = pl.BlockSpec(memory_space=pl.ANY)
SMEM = pl.BlockSpec(memory_space=pltpu.SMEM)
VMEM = pl.BlockSpec(memory_space=pltpu.VMEM)
HBM = pl.BlockSpec(memory_space=pltpu.HBM)
GROUP = 4
NOTE_ROWS = 16

HOME = 16


def swap(value, axis, size, bit):
    return lax.ppermute(value, axis, [(i, i ^ bit) for i in range(size)])


def pack_kernel(n_rel, where, note, *refs):
    halves, outs = refs[:n_rel], refs[n_rel:]
    rows, width = outs[0].shape[0] - NOTE_ROWS, outs[0].shape[1]
    first = pl.multiple_of(where[2, 0], rows)
    for j, out in enumerate(outs):
        start = pl.multiple_of(where[1, j], width)
        for r in range(n_rel):

            @pl.when(where[0, j] == r)
            def _(r=r, out=out, start=start):
                out[:rows] = halves[r][pl.ds(first, rows), pl.ds(start, width)]

        out[rows:] = note[...]


def gate_kernel(n_rel, rel, weight, bias, *refs):
    halves, out = refs[:n_rel], refs[n_rel]
    depth = halves[0].shape[1]
    total = jnp.zeros(out.shape, F32) + bias[...]
    for r, half in enumerate(halves):
        start = pl.multiple_of(lax.bitwise_xor(rel[0], r) * depth, depth)
        total += jnp.dot(half[...], weight[pl.ds(start, depth), :], preferred_element_type=F32)
    out[...] = jax.nn.sigmoid(total)


def stack_kernel(count, *refs):
    pieces, (out, notes) = refs[:count], refs[count:]
    rows = out.shape[1]
    for j, piece in enumerate(pieces):
        out[j] = piece[:rows]
        notes[j] = piece[rows:]


def take(refs, *counts):
    out = []
    for count in counts:
        out.append(refs[:count])
        refs = refs[count:]
    return out + [refs]


def start_tiles(way_counts, way, tiles, lists, sems):
    loads = []
    for g, count in enumerate(way_counts):
        options = [pltpu.make_async_copy(tiles[w], lists.at[g], sems.at[g]) for w in range(count)]
        tiles = tiles[count:]
        for w, option in enumerate(options):
            if count == 1:
                option.start()
            else:
                pl.when(way == w)(option.start)
        loads.append(options[0])
    return loads


def start_weights(members, member, weights, low, held, sems):
    half = members // 2
    loads = []
    for i, ref in enumerate(weights):
        block = ref.shape[1]
        start = pl.multiple_of(lax.bitwise_xor(i, member % half) * block, block)
        loads.append(
            pltpu.make_async_copy(
                ref, held.at[pl.ds(low, ref.shape[0]), pl.ds(start, block), :], sems.at[i]
            )
        )
        loads[-1].start()
    return loads


def multiply_tiles(turns, table, base, swapped, lists, rows_held, made):
    tile_rows = lists.shape[1]

    def step(n, _):
        for u in range(GROUP):
            s = n * GROUP + u
            first = pl.multiple_of(table[3, base + s], tile_rows)
            rows = rows_held[table[0, base + s], pl.ds(first, tile_rows), :]
            product = jnp.dot(lists[s], rows, preferred_element_type=F32)
            turned = pltpu.roll(product, product.shape[1] // 2, 1)
            made[s] = jnp.where(swapped, turned, product).astype(BF16)
        return 0

    lax.fori_loop(0, turns, step, 0)


def add_messages(turns, table, base, made, own, other, acc):
    acc[:-1] = jnp.zeros((acc.shape[0] - 1,) + acc.shape[1:], F32)

    def step(n, _):
        for u in range(GROUP):
            s = n * GROUP + u
            relation = table[2, base + s]
            weight = jnp.concatenate([own[relation], other[relation]], axis=0)
            acc[table[1, base + s]] += jnp.dot(made[s], weight, preferred_element_type=F32)
        return 0

    lax.fori_loop(0, turns, step, 0)


def put_messages(n_rel, rel, acc, outs):
    per_tile, tile_rows, features = acc.shape[0] - 1, acc.shape[1], acc.shape[2]
    own = features // n_rel
    for r in range(n_rel):
        start = pl.multiple_of(lax.bitwise_xor(rel, r) * own, own)
        for t in range(per_tile):
            outs[r][t * tile_rows:(t + 1) * tile_rows] = acc[t, :, pl.ds(start, own)].astype(outs[r].dtype)


def early_kernel(members, places, way_counts, table, *refs):
    half = members // 2
    states, tiles, weights, others, rest = take(refs, len(places), sum(way_counts), half, half)
    made, held, other, rows_held, lists, state_sem, tile_sem, weight_sem, other_sem = rest
    slots = lists.shape[1]
    chunks, rows = states[0].shape[0], states[0].shape[1]
    loads = []
    for n, ((i, r), ref) in enumerate(zip(places, states)):
        first = pl.multiple_of(lax.bitwise_xor(table[4, HOME + 1], r) * rows, rows)
        to = rows_held.at[pl.ds(i * chunks, chunks), pl.ds(first, rows), :]
        loads.append(pltpu.make_async_copy(ref, to, state_sem.at[n]))
        loads[-1].start()
    tile_loads = start_tiles(way_counts, table[4, HOME + 2], tiles, lists, tile_sem)
    weight_loads = start_weights(members, table[4, HOME], weights, 0, held, weight_sem)
    weight_loads += start_weights(members, table[4, HOME], others, 0, other, other_sem)
    for load in loads:
        load.wait()
    swapped = table[4, HOME] >= members // 2
    for j, load in enumerate(tile_loads):
        load.wait()
        multiply_tiles(table[4, j], table, j * slots, swapped, lists.at[j], rows_held, made.at[j])
    for load in weight_loads:
        load.wait()


def first_kernel(members, j, n_rel, table, made, own, begun, *refs):
    weights, outs, rest = take(refs, members // 2, n_rel)
    other, acc, weight_sem = rest
    del begun
    slots = made.shape[1]
    low = other.shape[0] - weights[0].shape[0]
    for load in start_weights(members, table[4, HOME], weights, low, other, weight_sem):
        load.wait()
    add_messages(table[4, j], table, j * slots, made.at[j], own, other, acc)
    put_messages(n_rel, table[4, HOME + 1], acc, outs)


def late_kernel(members, way_counts, js, n_rel, table, rows_held, own, other, *refs):
    tiles, outs, rest = take(refs, sum(way_counts), len(js) * n_rel)
    lists, made, acc, tile_sem = rest
    slots = lists.shape[1]
    loads = start_tiles(way_counts, table[4, HOME + 2], tiles, lists, tile_sem)
    for g, j in enumerate(js):
        loads[g].wait()
        multiply_tiles(
            table[4, j], table, j * slots, table[4, HOME] >= members // 2, lists.at[g], rows_held, made.at[g]
        )
        add_messages(table[4, j], table, j * slots, made.at[g], own, other, acc)
        put_messages(n_rel, table[4, HOME + 1], acc, outs[g * n_rel:(g + 1) * n_rel])


def near_kernel(js, n_rel, table, made, own, other, *refs):
    outs, acc = refs[:-1], refs[-1]
    slots = made.shape[1]
    for g, j in enumerate(js):
        add_messages(table[4, j], table, j * slots, made.at[j], own, other, acc)
        put_messages(n_rel, table[4, HOME + 1], acc, outs[g * n_rel:(g + 1) * n_rel])


def finish_kernel(used, state, gate_open, bias, *refs):
    terms, out = refs[:-1], refs[-1]
    message = sum(term[...].astype(F32) for term in terms[:-1])
    message = jnp.where(used[0] == 1, message + terms[-1][...].astype(F32), message)
    update = jnp.tanh(message + bias[...])
    opened = gate_open[...]
    out[...] = ((1.0 - opened) * state[...].astype(F32) + opened * update).astype(BF16)


def shards(
    n_rel, n_ent, chunks, state, rel_weight, gate_weight, gate_bias, update_bias,
    tile_values, tile_index, tile_count
):
    members = n_ent // chunks
    rel_dev, _, features = rel_weight.shape
    ent_dev, own_features = state.shape
    tile_rows = tile_values.shape[-1]
    slots = tile_values.shape[1]
    per_tile = ent_dev // tile_rows
    width = features // chunks
    rel = lax.axis_index("rel")
    ent = lax.axis_index("ent")
    part, member = ent // members, ent % members
    edge = jnp.logical_or(part == 0, part == chunks - 1).astype(jnp.int32)
    line = chunks == 4 and members == 4 and n_rel == 2

    def along(value, pairs):
        perm = [(a * members + m, b * members + m) for a, b in pairs for m in range(members)]
        return lax.ppermute(value, "ent", perm)

    def partner(value, j):
        return along(value, [(q, q ^ j) for q in range(chunks)])

    rows = ent_dev // n_rel
    halves = [state] + [swap(state, "rel", n_rel, r) for r in range(1, n_rel)]

    values = tile_values[0]
    if line:
        near = along(values, [(0, 1), (1, 0), (2, 3), (3, 2)])
        middle = along(values, [(1, 2), (2, 1)])
        onward = jnp.where(edge == 1, values, middle)
        two = along(onward, [(0, 2), (2, 3), (3, 1), (1, 0)])
        edge_three = along(two, [(2, 3), (1, 0)])
        tiles = [[values], [near], [two], [middle, edge_three]]
    else:
        tiles = [[values]] + [[partner(values, j)] for j in range(1, chunks)]

    note = jnp.zeros((NOTE_ROWS, width), BF16)
    note = note.at[:3, :slots].set(tile_index[0].astype(BF16))
    note = note.at[3, :1].set(tile_count[0].astype(BF16))
    asked = lax.bitwise_xor(part, jnp.arange(chunks, dtype=jnp.int32))
    per_half = chunks // n_rel
    where = jnp.stack([
        lax.bitwise_xor(asked // per_half, rel),
        (asked % per_half) * width,
        jnp.full((chunks,), rel * rows, jnp.int32),
    ])
    pieces = pl.pallas_call(
        functools.partial(pack_kernel, n_rel),
        out_shape=[jax.ShapeDtypeStruct((rows + NOTE_ROWS, width), BF16) for _ in range(chunks)],
        in_specs=[SMEM] + [VMEM] * (n_rel + 1),
        out_specs=[VMEM] * chunks,
        compiler_params=pltpu.CompilerParams(vmem_limit_bytes=8 << 20),
        name="pack",
    )(where, note, *halves)
    moved = [partner(pieces[j], j) for j in range(1, chunks)]
    own, notes = pl.pallas_call(
        functools.partial(stack_kernel, chunks),
        out_shape=[
            jax.ShapeDtypeStruct((chunks, rows, width), BF16),
            jax.ShapeDtypeStruct((chunks, NOTE_ROWS, width), BF16),
        ],
        in_specs=[VMEM] * chunks,
        out_specs=[VMEM] * 2,
        compiler_params=pltpu.CompilerParams(vmem_limit_bytes=8 << 20),
        name="stk",
    )(pieces[0], *moved)
    notes = notes[:, :4, :slots].astype(jnp.int32)
    counts = notes[:, 3, 0]
    source, target, relation = notes[:, 0], notes[:, 1], notes[:, 2]
    live = jnp.arange(slots, dtype=jnp.int32)[None] < counts[:, None]
    owner = source // per_tile
    place = lax.bitwise_xor(owner % members, member) * chunks
    place = place + lax.bitwise_xor(part, owner // members)
    turns = (counts + GROUP - 1) // GROUP
    last = jnp.zeros((chunks * slots,), jnp.int32).at[:chunks].set(turns)
    last = last.at[HOME:HOME + 3].set(jnp.stack([member, rel, edge]))
    table = jnp.stack([
        jnp.where(live, place, 0).reshape(-1),
        jnp.where(live, target, per_tile).reshape(-1),
        jnp.where(live, relation, 0).reshape(-1),
        (source % per_tile * tile_rows).reshape(-1),
        last,
    ])

    cut = max(1, rel_dev * 2 // 3)
    parts = (rel_weight[:cut], rel_weight[cut:])
    bits = [1 << b for b in reversed(range(members.bit_length() - 1))]
    rel_bits = [1 << b for b in reversed(range(n_rel.bit_length() - 1))]
    states, places = [own], [(0, 0)]

    def spread(axis, size, bit):
        more = [swap(v, axis, size, bit) for v in states]
        step = (0, bit) if axis == "rel" else (bit, 0)
        places.extend([(i | step[0], r | step[1]) for i, r in places])
        states.extend(more)

    for bit in bits[:-1]:
        spread("ent", n_ent, bit)
    for bit in rel_bits:
        spread("rel", n_rel, bit)
    spread("ent", n_ent, bits[-1])

    weights, order = [(rel_weight,)], [0]
    for bit in bits:
        more = []
        for i, held in enumerate(weights):
            if i == 0 and bit == bits[0]:
                more.append(tuple(swap(v, "ent", n_ent, bit) for v in parts))
            elif i == 0:
                more.append((swap(rel_weight, "ent", n_ent, bit),))
            else:
                more.append(tuple(swap(v, "ent", n_ent, bit) for v in held))
        weights = weights + more
        order = order + [o | bit for o in order]
    weights = [weights[order.index(i)] for i in range(members)]
    own_weights = [held[0] for held in weights[:members // 2]]
    other_weights = [[held[n] for held in weights[members // 2:]] for n in range(2)]

    gate_open = pl.pallas_call(
        functools.partial(gate_kernel, n_rel),
        out_shape=jax.ShapeDtypeStruct((ent_dev, own_features), F32),
        in_specs=[SMEM] + [VMEM] * (n_rel + 2),
        out_specs=VMEM,
        compiler_params=pltpu.CompilerParams(vmem_limit_bytes=12 << 20),
        name="gate",
    )(rel.reshape(1), gate_weight, gate_bias[None], *halves)

    early, late = tuple(range(3)), tuple(range(3, chunks))
    early_ways = [len(tiles[j]) for j in early]
    late_ways = [len(tiles[j]) for j in late]
    half_shape = (rel_dev, width // 2, features)
    products = jax.ShapeDtypeStruct((len(early), slots, tile_rows, width), BF16)
    acc_scratch = pltpu.VMEM((per_tile + 1, tile_rows, features), F32)

    def call(body, operands, in_specs, out_shape, scratch, flops, aliases=None):
        return pl.pallas_call(
            body,
            out_shape=out_shape,
            in_specs=[SMEM] + in_specs,
            out_specs=[VMEM] * len(out_shape),
            scratch_shapes=scratch,
            input_output_aliases=aliases or {},
            cost_estimate=pl.CostEstimate(
                flops=flops, bytes_accessed=rel_dev * width * features, transcendentals=0
            ),
            compiler_params=pltpu.CompilerParams(vmem_limit_bytes=20 << 20),
        )(table, *operands)

    def message_shapes(count):
        shape = (ent_dev, own_features)
        one = [jax.ShapeDtypeStruct(shape, F32)] + [jax.ShapeDtypeStruct(shape, BF16)] * (n_rel - 1)
        return one * count

    slot_flops = 2 * slots * tile_rows * width
    flat = [t for j in early for t in tiles[j]]
    operands = [*states, *flat, *own_weights, *other_weights[0]]
    made, own_half, begun, rows_held = call(
        functools.partial(early_kernel, members, tuple(places), early_ways),
        operands,
        [HBM if v is values or v is rel_weight else ANY for v in operands],
        [
            products,
            jax.ShapeDtypeStruct(half_shape, BF16),
            jax.ShapeDtypeStruct(half_shape, BF16),
            jax.ShapeDtypeStruct((members * chunks, ent_dev, width), BF16),
        ],
        [
            pltpu.VMEM((len(early), slots, tile_rows, tile_rows), BF16),
            pltpu.SemaphoreType.DMA((len(states),)),
            pltpu.SemaphoreType.DMA((len(early),)),
            pltpu.SemaphoreType.DMA((members // 2,)),
            pltpu.SemaphoreType.DMA((members // 2,)),
        ],
        len(early) * slot_flops * tile_rows,
    )
    *two, other_half = call(
        functools.partial(first_kernel, members, 2, n_rel),
        [made, own_half, begun, *other_weights[1]],
        [VMEM] * 3 + [ANY] * (members // 2),
        message_shapes(1) + [jax.ShapeDtypeStruct(half_shape, BF16)],
        [acc_scratch, pltpu.SemaphoreType.DMA((members // 2,))],
        slot_flops * features,
        {3: n_rel},
    )
    results = {2: two}
    for j in (1, 0):
        results[j] = call(
            functools.partial(near_kernel, (j,), n_rel),
            [made, own_half, other_half],
            [VMEM] * 3,
            message_shapes(1),
            [acc_scratch],
            slot_flops * features,
        )
    flat = [t for j in late for t in tiles[j]]
    rest = call(
        functools.partial(late_kernel, members, late_ways, late, n_rel),
        [rows_held, own_half, other_half, *flat],
        [VMEM] * 3 + [ANY] * len(flat),
        message_shapes(len(late)),
        [
            pltpu.VMEM((len(late), slots, tile_rows, tile_rows), BF16),
            pltpu.VMEM((len(late), slots, tile_rows, width), BF16),
            acc_scratch,
            pltpu.SemaphoreType.DMA((len(late),)),
        ],
        len(late) * slot_flops * (features + tile_rows),
    )
    for g, j in enumerate(late):
        results[j] = rest[g * n_rel:(g + 1) * n_rel]

    def summed(j, dtype=BF16):
        moved = [swap(v, "rel", n_rel, r + 1) for r, v in enumerate(results[j][1:])]
        term = results[j][0]
        for other in moved:
            term = term + other.astype(F32)
        return term.astype(dtype)

    if line:
        passed = along(summed(2), [(0, 1), (1, 3), (3, 2), (2, 0)])
        three = lax.optimization_barrier(summed(3))
        across = along(three, [(0, 3), (3, 0)])
        total = (three.astype(F32) + passed.astype(F32)).astype(BF16)
        total = along(total, [(1, 2), (2, 1)])
        terms = [summed(0, F32), partner(summed(1), 1), across, total, passed]
        used = edge
    else:
        terms = [summed(0, F32)]
        terms += [partner(summed(j), j) for j in range(1, chunks)]
        used = jnp.ones((), jnp.int32)
    return pl.pallas_call(
        finish_kernel,
        out_shape=jax.ShapeDtypeStruct((ent_dev, own_features), BF16),
        in_specs=[SMEM] + [VMEM] * (3 + len(terms)),
        out_specs=VMEM,
        compiler_params=pltpu.CompilerParams(vmem_limit_bytes=12 << 20),
        name="finish",
    )(used.reshape(1), state, gate_open, update_bias[None], *terms)


def solution(mesh):
    n_rel, n_ent = mesh.shape["rel"], mesh.shape["ent"]
    chunks = max(4, n_rel)
    in_specs = (
        P("ent", "rel"),
        P("rel", "ent", None),
        P(None, "rel"),
        P("rel"),
        P("rel"),
        P("rel", "ent", None, None),
        P("rel", None, "ent"),
        P("rel", "ent"),
    )
    return jax.shard_map(
        functools.partial(shards, n_rel, n_ent, chunks),
        mesh=mesh, in_specs=in_specs, out_specs=P("ent", "rel"), check_vma=False,
    )
```

```python
import functools

import jax
import jax.numpy as jnp
from jax import lax
from jax.experimental import pallas as pl
from jax.experimental.pallas import tpu as pltpu
from jax.sharding import PartitionSpec as P


F32 = jnp.float32
BF16 = jnp.bfloat16
ANY = pl.BlockSpec(memory_space=pl.ANY)
SMEM = pl.BlockSpec(memory_space=pltpu.SMEM)
VMEM = pl.BlockSpec(memory_space=pltpu.VMEM)
HBM = pl.BlockSpec(memory_space=pltpu.HBM)
GROUP = 4
NOTE_ROWS = 16

HOME = 16


def swap(value, axis, size, bit):
    return lax.ppermute(value, axis, [(i, i ^ bit) for i in range(size)])


def pack_kernel(n_rel, where, note, *refs):
    halves, outs = refs[:n_rel], refs[n_rel:]
    rows, width = outs[0].shape[0] - NOTE_ROWS, outs[0].shape[1]
    first = pl.multiple_of(where[2, 0], rows)
    for j, out in enumerate(outs):
        start = pl.multiple_of(where[1, j], width)
        for r in range(n_rel):

            @pl.when(where[0, j] == r)
            def _(r=r, out=out, start=start):
                out[:rows] = halves[r][pl.ds(first, rows), pl.ds(start, width)]

        out[rows:] = note[...]


def gate_kernel(n_rel, rel, weight, bias, *refs):
    halves, out = refs[:n_rel], refs[n_rel]
    depth = halves[0].shape[1]
    total = jnp.zeros(out.shape, F32) + bias[...]
    for r, half in enumerate(halves):
        start = pl.multiple_of(lax.bitwise_xor(rel[0], r) * depth, depth)
        total += jnp.dot(half[...], weight[pl.ds(start, depth), :], preferred_element_type=F32)
    out[...] = jax.nn.sigmoid(total)


def stack_kernel(count, *refs):
    pieces, (out, notes) = refs[:count], refs[count:]
    rows = out.shape[1]
    for j, piece in enumerate(pieces):
        out[j] = piece[:rows]
        notes[j] = piece[rows:]


def take(refs, *counts):
    out = []
    for count in counts:
        out.append(refs[:count])
        refs = refs[count:]
    return out + [refs]


def start_tiles(way_counts, way, tiles, lists, sems):
    loads = []
    for g, count in enumerate(way_counts):
        options = [pltpu.make_async_copy(tiles[w], lists.at[g], sems.at[g]) for w in range(count)]
        tiles = tiles[count:]
        for w, option in enumerate(options):
            if count == 1:
                option.start()
            else:
                pl.when(way == w)(option.start)
        loads.append(options[0])
    return loads


def start_weights(members, member, weights, low, held, sems):
    half = members // 2
    loads = []
    for i, ref in enumerate(weights):
        block = ref.shape[1]
        start = pl.multiple_of(lax.bitwise_xor(i, member % half) * block, block)
        loads.append(
            pltpu.make_async_copy(
                ref, held.at[pl.ds(low, ref.shape[0]), pl.ds(start, block), :], sems.at[i]
            )
        )
        loads[-1].start()
    return loads


def multiply_tiles(turns, table, base, swapped, lists, rows_held, made):
    tile_rows = lists.shape[1]

    def step(n, _):
        for u in range(GROUP):
            s = n * GROUP + u
            first = pl.multiple_of(table[3, base + s], tile_rows)
            rows = rows_held[table[0, base + s], pl.ds(first, tile_rows), :]
            product = jnp.dot(lists[s], rows, preferred_element_type=F32)
            turned = pltpu.roll(product, product.shape[1] // 2, 1)
            made[s] = jnp.where(swapped, turned, product).astype(BF16)
        return 0

    lax.fori_loop(0, turns, step, 0)


def add_messages(turns, table, base, made, own, other, acc):
    acc[:-1] = jnp.zeros((acc.shape[0] - 1,) + acc.shape[1:], F32)

    def step(n, _):
        for u in range(GROUP):
            s = n * GROUP + u
            relation = table[2, base + s]
            weight = jnp.concatenate([own[relation], other[relation]], axis=0)
            acc[table[1, base + s]] += jnp.dot(made[s], weight, preferred_element_type=F32)
        return 0

    lax.fori_loop(0, turns, step, 0)


def put_messages(n_rel, rel, acc, outs):
    per_tile, tile_rows, features = acc.shape[0] - 1, acc.shape[1], acc.shape[2]
    own = features // n_rel
    for r in range(n_rel):
        start = pl.multiple_of(lax.bitwise_xor(rel, r) * own, own)
        for t in range(per_tile):
            outs[r][t * tile_rows:(t + 1) * tile_rows] = acc[t, :, pl.ds(start, own)].astype(outs[r].dtype)


def early_kernel(members, places, way_counts, table, *refs):
    half = members // 2
    states, tiles, weights, others, rest = take(refs, len(places), sum(way_counts), half, half)
    made, held, other, rows_held, lists, state_sem, tile_sem, weight_sem, other_sem = rest
    slots = lists.shape[1]
    chunks, rows = states[0].shape[0], states[0].shape[1]
    loads = []
    for n, ((i, r), ref) in enumerate(zip(places, states)):
        first = pl.multiple_of(lax.bitwise_xor(table[4, HOME + 1], r) * rows, rows)
        to = rows_held.at[pl.ds(i * chunks, chunks), pl.ds(first, rows), :]
        loads.append(pltpu.make_async_copy(ref, to, state_sem.at[n]))
        loads[-1].start()
    tile_loads = start_tiles(way_counts, table[4, HOME + 2], tiles, lists, tile_sem)
    weight_loads = start_weights(members, table[4, HOME], weights, 0, held, weight_sem)
    weight_loads += start_weights(members, table[4, HOME], others, 0, other, other_sem)
    for load in loads:
        load.wait()
    swapped = table[4, HOME] >= members // 2
    for j, load in enumerate(tile_loads):
        load.wait()
        multiply_tiles(table[4, j], table, j * slots, swapped, lists.at[j], rows_held, made.at[j])
    for load in weight_loads:
        load.wait()


def first_kernel(members, j, n_rel, table, made, own, begun, *refs):
    weights, outs, rest = take(refs, members // 2, n_rel)
    other, acc, weight_sem = rest
    del begun
    slots = made.shape[1]
    low = other.shape[0] - weights[0].shape[0]
    for load in start_weights(members, table[4, HOME], weights, low, other, weight_sem):
        load.wait()
    add_messages(table[4, j], table, j * slots, made.at[j], own, other, acc)
    put_messages(n_rel, table[4, HOME + 1], acc, outs)


def late_kernel(members, way_counts, js, n_rel, table, rows_held, own, other, *refs):
    tiles, outs, rest = take(refs, sum(way_counts), len(js) * n_rel)
    lists, made, acc, tile_sem = rest
    slots = lists.shape[1]
    loads = start_tiles(way_counts, table[4, HOME + 2], tiles, lists, tile_sem)
    for g, j in enumerate(js):
        loads[g].wait()
        multiply_tiles(
            table[4, j], table, j * slots, table[4, HOME] >= members // 2, lists.at[g], rows_held, made.at[g]
        )
        add_messages(table[4, j], table, j * slots, made.at[g], own, other, acc)
        put_messages(n_rel, table[4, HOME + 1], acc, outs[g * n_rel:(g + 1) * n_rel])


def near_kernel(js, n_rel, table, made, own, other, *refs):
    outs, acc = refs[:-1], refs[-1]
    slots = made.shape[1]
    for g, j in enumerate(js):
        add_messages(table[4, j], table, j * slots, made.at[j], own, other, acc)
        put_messages(n_rel, table[4, HOME + 1], acc, outs[g * n_rel:(g + 1) * n_rel])


def finish_kernel(used, state, gate_open, bias, *refs):
    terms, out = refs[:-1], refs[-1]
    message = sum(term[...].astype(F32) for term in terms[:-1])
    message = jnp.where(used[0] == 1, message + terms[-1][...].astype(F32), message)
    update = jnp.tanh(message + bias[...])
    opened = gate_open[...]
    out[...] = ((1.0 - opened) * state[...].astype(F32) + opened * update).astype(BF16)


def shards(
    n_rel, n_ent, chunks, state, rel_weight, gate_weight, gate_bias, update_bias,
    tile_values, tile_index, tile_count
):
    members = n_ent // chunks
    rel_dev, _, features = rel_weight.shape
    ent_dev, own_features = state.shape
    tile_rows = tile_values.shape[-1]
    slots = tile_values.shape[1]
    per_tile = ent_dev // tile_rows
    width = features // chunks
    rel = lax.axis_index("rel")
    ent = lax.axis_index("ent")
    part, member = ent // members, ent % members
    edge = jnp.logical_or(part == 0, part == chunks - 1).astype(jnp.int32)
    line = chunks == 4 and members == 4 and n_rel == 2

    def along(value, pairs):
        perm = [(a * members + m, b * members + m) for a, b in pairs for m in range(members)]
        return lax.ppermute(value, "ent", perm)

    def partner(value, j):
        return along(value, [(q, q ^ j) for q in range(chunks)])

    rows = ent_dev // n_rel
    halves = [state] + [swap(state, "rel", n_rel, r) for r in range(1, n_rel)]

    values = tile_values[0]
    if line:
        near = along(values, [(0, 1), (1, 0), (2, 3), (3, 2)])
        middle = along(values, [(1, 2), (2, 1)])
        onward = jnp.where(edge == 1, values, middle)
        two = along(onward, [(0, 2), (2, 3), (3, 1), (1, 0)])
        edge_three = along(two, [(2, 3), (1, 0)])
        tiles = [[values], [near], [two], [middle, edge_three]]
    else:
        tiles = [[values]] + [[partner(values, j)] for j in range(1, chunks)]

    note = jnp.zeros((NOTE_ROWS, width), BF16)
    note = note.at[:3, :slots].set(tile_index[0].astype(BF16))
    note = note.at[3, :1].set(tile_count[0].astype(BF16))
    asked = lax.bitwise_xor(part, jnp.arange(chunks, dtype=jnp.int32))
    per_half = chunks // n_rel
    where = jnp.stack([
        lax.bitwise_xor(asked // per_half, rel),
        (asked % per_half) * width,
        jnp.full((chunks,), rel * rows, jnp.int32),
    ])
    pieces = pl.pallas_call(
        functools.partial(pack_kernel, n_rel),
        out_shape=[jax.ShapeDtypeStruct((rows + NOTE_ROWS, width), BF16) for _ in range(chunks)],
        in_specs=[SMEM] + [VMEM] * (n_rel + 1),
        out_specs=[VMEM] * chunks,
        compiler_params=pltpu.CompilerParams(vmem_limit_bytes=8 << 20),
        name="pack",
    )(where, note, *halves)
    moved = [partner(pieces[j], j) for j in range(1, chunks)]
    own, notes = pl.pallas_call(
        functools.partial(stack_kernel, chunks),
        out_shape=[
            jax.ShapeDtypeStruct((chunks, rows, width), BF16),
            jax.ShapeDtypeStruct((chunks, NOTE_ROWS, width), BF16),
        ],
        in_specs=[VMEM] * chunks,
        out_specs=[VMEM] * 2,
        compiler_params=pltpu.CompilerParams(vmem_limit_bytes=8 << 20),
        name="stk",
    )(pieces[0], *moved)
    notes = notes[:, :4, :slots].astype(jnp.int32)
    counts = notes[:, 3, 0]
    source, target, relation = notes[:, 0], notes[:, 1], notes[:, 2]
    live = jnp.arange(slots, dtype=jnp.int32)[None] < counts[:, None]
    owner = source // per_tile
    place = lax.bitwise_xor(owner % members, member) * chunks
    place = place + lax.bitwise_xor(part, owner // members)
    turns = (counts + GROUP - 1) // GROUP
    last = jnp.zeros((chunks * slots,), jnp.int32).at[:chunks].set(turns)
    last = last.at[HOME:HOME + 3].set(jnp.stack([member, rel, edge]))
    table = jnp.stack([
        jnp.where(live, place, 0).reshape(-1),
        jnp.where(live, target, per_tile).reshape(-1),
        jnp.where(live, relation, 0).reshape(-1),
        (source % per_tile * tile_rows).reshape(-1),
        last,
    ])

    cut = max(1, rel_dev * 7 // 12)
    parts = [rel_weight[:cut]]
    parts.append(rel_weight[cut:])
    bits = [1 << b for b in reversed(range(members.bit_length() - 1))]
    rel_bits = [1 << b for b in reversed(range(n_rel.bit_length() - 1))]
    states, places = [own], [(0, 0)]

    def spread(axis, size, bit):
        more = [swap(v, axis, size, bit) for v in states]
        step = (0, bit) if axis == "rel" else (bit, 0)
        places.extend([(i | step[0], r | step[1]) for i, r in places])
        states.extend(more)

    for bit in bits[:-1]:
        spread("ent", n_ent, bit)
    for bit in rel_bits:
        spread("rel", n_rel, bit)
    spread("ent", n_ent, bits[-1])

    weights, order = [(rel_weight,)], [0]
    for bit in bits:
        more = []
        for i, held in enumerate(weights):
            if i == 0 and bit == bits[0]:
                more.append(tuple(swap(v, "ent", n_ent, bit) for v in parts))
            elif i == 0:
                more.append((swap(rel_weight, "ent", n_ent, bit),))
            else:
                more.append(tuple(swap(v, "ent", n_ent, bit) for v in held))
        weights = weights + more
        order = order + [o | bit for o in order]
    weights = [weights[order.index(i)] for i in range(members)]
    own_weights = [held[0] for held in weights[:members // 2]]
    other_weights = [[held[n] for held in weights[members // 2:]] for n in range(2)]

    gate_open = pl.pallas_call(
        functools.partial(gate_kernel, n_rel),
        out_shape=jax.ShapeDtypeStruct((ent_dev, own_features), F32),
        in_specs=[SMEM] + [VMEM] * (n_rel + 2),
        out_specs=VMEM,
        compiler_params=pltpu.CompilerParams(vmem_limit_bytes=12 << 20),
        name="gate",
    )(rel.reshape(1), gate_weight, gate_bias[None], *halves)

    early, late = tuple(range(3)), tuple(range(3, chunks))
    early_ways = [len(tiles[j]) for j in early]
    late_ways = [len(tiles[j]) for j in late]
    half_shape = (rel_dev, width // 2, features)
    products = jax.ShapeDtypeStruct((len(early), slots, tile_rows, width), BF16)
    acc_scratch = pltpu.VMEM((per_tile + 1, tile_rows, features), F32)

    def call(body, operands, in_specs, out_shape, scratch, flops, aliases=None):
        return pl.pallas_call(
            body,
            out_shape=out_shape,
            in_specs=[SMEM] + in_specs,
            out_specs=[VMEM] * len(out_shape),
            scratch_shapes=scratch,
            input_output_aliases=aliases or {},
            cost_estimate=pl.CostEstimate(
                flops=flops, bytes_accessed=rel_dev * width * features, transcendentals=0
            ),
            compiler_params=pltpu.CompilerParams(vmem_limit_bytes=20 << 20),
        )(table, *operands)

    def message_shapes(count):
        shape = (ent_dev, own_features)
        one = [jax.ShapeDtypeStruct(shape, F32)] + [jax.ShapeDtypeStruct(shape, BF16)] * (n_rel - 1)
        return one * count

    slot_flops = 2 * slots * tile_rows * width
    flat = [t for j in early for t in tiles[j]]
    operands = [*states, *flat, *own_weights, *other_weights[0]]
    made, own_half, begun, rows_held = call(
        functools.partial(early_kernel, members, tuple(places), early_ways),
        operands,
        [HBM if v is values or v is rel_weight else ANY for v in operands],
        [
            products,
            jax.ShapeDtypeStruct(half_shape, BF16),
            jax.ShapeDtypeStruct(half_shape, BF16),
            jax.ShapeDtypeStruct((members * chunks, ent_dev, width), BF16),
        ],
        [
            pltpu.VMEM((len(early), slots, tile_rows, tile_rows), BF16),
            pltpu.SemaphoreType.DMA((len(states),)),
            pltpu.SemaphoreType.DMA((len(early),)),
            pltpu.SemaphoreType.DMA((members // 2,)),
            pltpu.SemaphoreType.DMA((members // 2,)),
        ],
        len(early) * slot_flops * tile_rows,
    )
    *two, other_half = call(
        functools.partial(first_kernel, members, 2, n_rel),
        [made, own_half, begun, *other_weights[1]],
        [VMEM] * 3 + [ANY] * (members // 2),
        message_shapes(1) + [jax.ShapeDtypeStruct(half_shape, BF16)],
        [acc_scratch, pltpu.SemaphoreType.DMA((members // 2,))],
        slot_flops * features,
        {3: n_rel},
    )
    results = {2: two}
    for j in (1, 0):
        results[j] = call(
            functools.partial(near_kernel, (j,), n_rel),
            [made, own_half, other_half],
            [VMEM] * 3,
            message_shapes(1),
            [acc_scratch],
            slot_flops * features,
        )
    flat = [t for j in late for t in tiles[j]]
    rest = call(
        functools.partial(late_kernel, members, late_ways, late, n_rel),
        [rows_held, own_half, other_half, *flat],
        [VMEM] * 3 + [ANY] * len(flat),
        message_shapes(len(late)),
        [
            pltpu.VMEM((len(late), slots, tile_rows, tile_rows), BF16),
            pltpu.VMEM((len(late), slots, tile_rows, width), BF16),
            acc_scratch,
            pltpu.SemaphoreType.DMA((len(late),)),
        ],
        len(late) * slot_flops * (features + tile_rows),
    )
    for g, j in enumerate(late):
        results[j] = rest[g * n_rel:(g + 1) * n_rel]

    def summed(j, dtype=BF16):
        moved = [swap(v, "rel", n_rel, r + 1) for r, v in enumerate(results[j][1:])]
        term = results[j][0]
        for other in moved:
            term = term + other.astype(F32)
        return term.astype(dtype)

    if line:
        passed = along(summed(2), [(0, 1), (1, 3), (3, 2), (2, 0)])
        three = lax.optimization_barrier(summed(3))
        across = along(three, [(0, 3), (3, 0)])
        total = (three.astype(F32) + passed.astype(F32)).astype(BF16)
        total = along(total, [(1, 2), (2, 1)])
        terms = [summed(0, F32), partner(summed(1), 1), across, total, passed]
        used = edge
    else:
        terms = [summed(0, F32)]
        terms += [partner(summed(j), j) for j in range(1, chunks)]
        used = jnp.ones((), jnp.int32)
    return pl.pallas_call(
        finish_kernel,
        out_shape=jax.ShapeDtypeStruct((ent_dev, own_features), BF16),
        in_specs=[SMEM] + [VMEM] * (3 + len(terms)),
        out_specs=VMEM,
        compiler_params=pltpu.CompilerParams(vmem_limit_bytes=12 << 20),
        name="finish",
    )(used.reshape(1), state, gate_open, update_bias[None], *terms)


def solution(mesh):
    n_rel, n_ent = mesh.shape["rel"], mesh.shape["ent"]
    chunks = max(4, n_rel)
    in_specs = (
        P("ent", "rel"),
        P("rel", "ent", None),
        P(None, "rel"),
        P("rel"),
        P("rel"),
        P("rel", "ent", None, None),
        P("rel", None, "ent"),
        P("rel", "ent"),
    )
    return jax.shard_map(
        functools.partial(shards, n_rel, n_ent, chunks),
        mesh=mesh, in_specs=in_specs, out_specs=P("ent", "rel"), check_vma=False,
    )
```

```python
import functools

import jax
import jax.numpy as jnp
from jax import lax
from jax.experimental import pallas as pl
from jax.experimental.pallas import tpu as pltpu
from jax.sharding import PartitionSpec as P


F32 = jnp.float32
BF16 = jnp.bfloat16
ANY = pl.BlockSpec(memory_space=pl.ANY)
SMEM = pl.BlockSpec(memory_space=pltpu.SMEM)
VMEM = pl.BlockSpec(memory_space=pltpu.VMEM)
HBM = pl.BlockSpec(memory_space=pltpu.HBM)
GROUP = 4
NOTE_ROWS = 16

PLACE, TARGET, RELATION, FIRST, TURNS, MEMBER, REL, EDGE = range(8)
LANES = 128


def swap(value, axis, size, bit):
    return lax.ppermute(value, axis, [(i, i ^ bit) for i in range(size)])


def pack_kernel(n_rel, where, note, *refs):
    halves, outs, sems = refs[:n_rel], refs[n_rel:-1], refs[-1]
    rows, width = outs[0].shape[0] - NOTE_ROWS, outs[0].shape[1]
    first = pl.multiple_of(where[2, 0], rows)
    copies = []
    for j, out in enumerate(outs):
        start = pl.multiple_of(where[1, j], width)
        options = [
            pltpu.make_async_copy(
                half.at[pl.ds(first, rows), pl.ds(start, width)], out.at[pl.ds(0, rows), :], sems.at[j]
            )
            for half in halves
        ]
        for r, option in enumerate(options):
            pl.when(where[0, j] == r)(option.start)
        copies.append(options[0])
    for out in outs:
        out[rows:] = note[...]
    for copy in copies:
        copy.wait()


def gate_kernel(n_rel, rel, weight, bias, *refs):
    halves, out = refs[:n_rel], refs[n_rel]
    depth = halves[0].shape[1]
    total = jnp.zeros(out.shape, F32) + bias[...]
    for r, half in enumerate(halves):
        start = pl.multiple_of(lax.bitwise_xor(rel[0], r) * depth, depth)
        total += jnp.dot(half[...], weight[pl.ds(start, depth), :], preferred_element_type=F32)
    out[...] = jax.nn.sigmoid(total)


def stack_kernel(count, sizes, here, *refs):
    pieces, (out, table) = refs[:count], refs[count:]
    members, per_tile, tile_rows, slots = sizes
    part, member = here[0], here[1]
    rows = out.shape[1]
    tile_bits, member_bits = per_tile.bit_length() - 1, members.bit_length() - 1
    lane = lax.broadcasted_iota(jnp.int32, (1, LANES), 1)
    for j, piece in enumerate(pieces):
        out[j] = piece[:rows]
        note = piece[rows:, :LANES].astype(F32).astype(jnp.int32)
        source, live_total = note[0:1], note[3:4]
        live = jnp.logical_and(lane < live_total, lane < slots)
        owner = lax.shift_right_logical(source, tile_bits)
        place = lax.bitwise_xor(owner & (members - 1), member) * count
        place = place + lax.bitwise_xor(lax.shift_right_logical(owner, member_bits), part)
        values = {
            PLACE: jnp.where(live, place, 0),
            TARGET: jnp.where(live, note[1:2], per_tile),
            RELATION: jnp.where(live, note[2:3], 0),
            FIRST: jnp.where(live, (source & (per_tile - 1)) * tile_rows, 0),
            TURNS: lax.shift_right_logical(live_total + (GROUP - 1), GROUP.bit_length() - 1),
            MEMBER: jnp.full((1, LANES), member, jnp.int32),
            REL: jnp.full((1, LANES), here[2], jnp.int32),
            EDGE: jnp.full((1, LANES), here[3], jnp.int32),
        }
        for row, value in values.items():
            table[8 * j + row:8 * j + row + 1, :] = value


def take(refs, *counts):
    out = []
    for count in counts:
        out.append(refs[:count])
        refs = refs[count:]
    return out + [refs]


def start_tiles(way_counts, way, tiles, lists, sems):
    loads = []
    for g, count in enumerate(way_counts):
        options = [pltpu.make_async_copy(tiles[w], lists.at[g], sems.at[g]) for w in range(count)]
        tiles = tiles[count:]
        for w, option in enumerate(options):
            if count == 1:
                option.start()
            else:
                pl.when(way == w)(option.start)
        loads.append(options[0])
    return loads


def start_weights(members, member, weights, low, held, sems):
    half = members // 2
    loads = []
    for i, ref in enumerate(weights):
        block = ref.shape[1]
        start = pl.multiple_of(lax.bitwise_xor(i, member % half) * block, block)
        loads.append(
            pltpu.make_async_copy(
                ref, held.at[pl.ds(low, ref.shape[0]), pl.ds(start, block), :], sems.at[i]
            )
        )
        loads[-1].start()
    return loads


def multiply_tiles(table, j, swapped, lists, rows_held, made):
    tile_rows = lists.shape[1]

    def step(n, _):
        for u in range(GROUP):
            s = n * GROUP + u
            first = pl.multiple_of(table[8 * j + FIRST, s], tile_rows)
            rows = rows_held[table[8 * j + PLACE, s], pl.ds(first, tile_rows), :]
            product = jnp.dot(lists[s], rows, preferred_element_type=F32)
            turned = pltpu.roll(product, product.shape[1] // 2, 1)
            made[s] = jnp.where(swapped, turned, product).astype(BF16)
        return 0

    lax.fori_loop(0, table[8 * j + TURNS, 0], step, 0)


def add_messages(table, j, made, own, other, acc):
    acc[:-1] = jnp.zeros((acc.shape[0] - 1,) + acc.shape[1:], F32)

    def step(n, _):
        for u in range(GROUP):
            s = n * GROUP + u
            relation = table[8 * j + RELATION, s]
            weight = jnp.concatenate([own[relation], other[relation]], axis=0)
            acc[table[8 * j + TARGET, s]] += jnp.dot(made[s], weight, preferred_element_type=F32)
        return 0

    lax.fori_loop(0, table[8 * j + TURNS, 0], step, 0)


def put_messages(n_rel, rel, acc, outs):
    per_tile, tile_rows, features = acc.shape[0] - 1, acc.shape[1], acc.shape[2]
    own = features // n_rel
    for r in range(n_rel):
        start = pl.multiple_of(lax.bitwise_xor(rel, r) * own, own)
        for t in range(per_tile):
            outs[r][t * tile_rows:(t + 1) * tile_rows] = acc[t, :, pl.ds(start, own)].astype(outs[r].dtype)


def early_kernel(members, places, way_counts, table, *refs):
    half = members // 2
    states, tiles, weights, others, rest = take(refs, len(places), sum(way_counts), half, half)
    made, held, other, rows_held, lists, state_sem, tile_sem, weight_sem, other_sem = rest
    chunks, rows = states[0].shape[0], states[0].shape[1]
    loads = []
    for n, ((i, r), ref) in enumerate(zip(places, states)):
        first = pl.multiple_of(lax.bitwise_xor(table[REL, 0], r) * rows, rows)
        to = rows_held.at[pl.ds(i * chunks, chunks), pl.ds(first, rows), :]
        loads.append(pltpu.make_async_copy(ref, to, state_sem.at[n]))
        loads[-1].start()
    tile_loads = start_tiles(way_counts, table[EDGE, 0], tiles, lists, tile_sem)
    weight_loads = start_weights(members, table[MEMBER, 0], weights, 0, held, weight_sem)
    weight_loads += start_weights(members, table[MEMBER, 0], others, 0, other, other_sem)
    for load in loads:
        load.wait()
    swapped = table[MEMBER, 0] >= members // 2
    for j, load in enumerate(tile_loads):
        load.wait()
        multiply_tiles(table, j, swapped, lists.at[j], rows_held, made.at[j])
    for load in weight_loads:
        load.wait()


def first_kernel(members, j, n_rel, table, made, own, begun, *refs):
    weights, outs, rest = take(refs, members // 2, n_rel)
    other, acc, weight_sem = rest
    del begun
    low = other.shape[0] - weights[0].shape[0]
    for load in start_weights(members, table[MEMBER, 0], weights, low, other, weight_sem):
        load.wait()
    add_messages(table, j, made.at[j], own, other, acc)
    put_messages(n_rel, table[REL, 0], acc, outs)


def late_kernel(members, way_counts, js, n_rel, table, rows_held, own, other, *refs):
    tiles, outs, rest = take(refs, sum(way_counts), len(js) * n_rel)
    lists, made, acc, tile_sem = rest
    loads = start_tiles(way_counts, table[EDGE, 0], tiles, lists, tile_sem)
    for g, j in enumerate(js):
        loads[g].wait()
        multiply_tiles(table, j, table[MEMBER, 0] >= members // 2, lists.at[g], rows_held, made.at[g])
        add_messages(table, j, made.at[g], own, other, acc)
        put_messages(n_rel, table[REL, 0], acc, outs[g * n_rel:(g + 1) * n_rel])


def near_kernel(js, n_rel, table, made, own, other, *refs):
    outs, acc = refs[:-1], refs[-1]
    for g, j in enumerate(js):
        add_messages(table, j, made.at[j], own, other, acc)
        put_messages(n_rel, table[REL, 0], acc, outs[g * n_rel:(g + 1) * n_rel])


def finish_kernel(used, state, gate_open, bias, *refs):
    terms, out = refs[:-1], refs[-1]
    message = sum(term[...].astype(F32) for term in terms[:-1])
    message = jnp.where(used[0] == 1, message + terms[-1][...].astype(F32), message)
    update = jnp.tanh(message + bias[...])
    opened = gate_open[...]
    out[...] = ((1.0 - opened) * state[...].astype(F32) + opened * update).astype(BF16)


def shards(
    n_rel, n_ent, chunks, state, rel_weight, gate_weight, gate_bias, update_bias,
    tile_values, tile_index, tile_count
):
    members = n_ent // chunks
    rel_dev, _, features = rel_weight.shape
    ent_dev, own_features = state.shape
    tile_rows = tile_values.shape[-1]
    slots = tile_values.shape[1]
    per_tile = ent_dev // tile_rows
    width = features // chunks
    rel = lax.axis_index("rel")
    ent = lax.axis_index("ent")
    part, member = ent // members, ent % members
    edge = jnp.logical_or(part == 0, part == chunks - 1).astype(jnp.int32)
    line = chunks == 4 and members == 4 and n_rel == 2

    def along(value, pairs):
        perm = [(a * members + m, b * members + m) for a, b in pairs for m in range(members)]
        return lax.ppermute(value, "ent", perm)

    def partner(value, j):
        return along(value, [(q, q ^ j) for q in range(chunks)])

    rows = ent_dev // n_rel
    halves = [state] + [swap(state, "rel", n_rel, r) for r in range(1, n_rel)]

    values = tile_values[0]
    if line:
        near = along(values, [(0, 1), (1, 0), (2, 3), (3, 2)])
        middle = along(values, [(1, 2), (2, 1)])
        onward = jnp.where(edge == 1, values, middle)
        two = along(onward, [(0, 2), (2, 3), (3, 1), (1, 0)])
        edge_three = along(two, [(2, 3), (1, 0)])
        tiles = [[values], [near], [two], [middle, edge_three]]
    else:
        tiles = [[values]] + [[partner(values, j)] for j in range(1, chunks)]

    note = jnp.zeros((NOTE_ROWS, width), BF16)
    note = note.at[:3, :slots].set(tile_index[0].astype(BF16))
    note = note.at[3].set(tile_count[0, 0].astype(BF16))
    asked = lax.bitwise_xor(part, jnp.arange(chunks, dtype=jnp.int32))
    per_half = chunks // n_rel
    where = jnp.stack([
        lax.bitwise_xor(asked // per_half, rel),
        (asked % per_half) * width,
        jnp.full((chunks,), rel * rows, jnp.int32),
    ])
    pieces = pl.pallas_call(
        functools.partial(pack_kernel, n_rel),
        out_shape=[jax.ShapeDtypeStruct((rows + NOTE_ROWS, width), BF16) for _ in range(chunks)],
        in_specs=[SMEM, VMEM] + [HBM] * n_rel,
        out_specs=[VMEM] * chunks,
        scratch_shapes=[pltpu.SemaphoreType.DMA((chunks,))],
        compiler_params=pltpu.CompilerParams(vmem_limit_bytes=8 << 20),
        name="pack",
    )(where, note, *halves)
    moved = [partner(pieces[j], j) for j in range(1, chunks)]
    assert per_tile & (per_tile - 1) == 0 and members & (members - 1) == 0 and slots <= LANES <= width
    here = jnp.stack([part, member, rel, edge])
    own, table = pl.pallas_call(
        functools.partial(stack_kernel, chunks, (members, per_tile, tile_rows, slots)),
        out_shape=[
            jax.ShapeDtypeStruct((chunks, rows, width), BF16),
            jax.ShapeDtypeStruct((8 * chunks, LANES), jnp.int32),
        ],
        in_specs=[SMEM] + [VMEM] * chunks,
        out_specs=[VMEM] * 2,
        compiler_params=pltpu.CompilerParams(vmem_limit_bytes=8 << 20),
        name="stk",
    )(here, pieces[0], *moved)

    cut = max(1, rel_dev * 2 // 3)
    parts = [rel_weight[:cut]]
    parts.append(rel_weight[cut:])
    bits = [1 << b for b in reversed(range(members.bit_length() - 1))]
    rel_bits = [1 << b for b in reversed(range(n_rel.bit_length() - 1))]
    states, places = [own], [(0, 0)]

    def spread(axis, size, bit):
        more = [swap(v, axis, size, bit) for v in states]
        step = (0, bit) if axis == "rel" else (bit, 0)
        places.extend([(i | step[0], r | step[1]) for i, r in places])
        states.extend(more)

    for bit in bits[:-1]:
        spread("ent", n_ent, bit)
    for bit in rel_bits:
        spread("rel", n_rel, bit)
    spread("ent", n_ent, bits[-1])

    weights, order = [(rel_weight,)], [0]
    for bit in bits:
        more = []
        for i, held in enumerate(weights):
            if i == 0 and bit == bits[0]:
                more.append(tuple(swap(v, "ent", n_ent, bit) for v in parts))
            elif i == 0:
                more.append((swap(rel_weight, "ent", n_ent, bit),))
            else:
                more.append(tuple(swap(v, "ent", n_ent, bit) for v in held))
        weights = weights + more
        order = order + [o | bit for o in order]
    weights = [weights[order.index(i)] for i in range(members)]
    own_weights = [held[0] for held in weights[:members // 2]]
    other_weights = [[held[n] for held in weights[members // 2:]] for n in range(2)]

    gate_open = pl.pallas_call(
        functools.partial(gate_kernel, n_rel),
        out_shape=jax.ShapeDtypeStruct((ent_dev, own_features), F32),
        in_specs=[SMEM] + [VMEM] * (n_rel + 2),
        out_specs=VMEM,
        compiler_params=pltpu.CompilerParams(vmem_limit_bytes=12 << 20),
        name="gate",
    )(rel.reshape(1), gate_weight, gate_bias[None], *halves)

    early, late = tuple(range(3)), tuple(range(3, chunks))
    early_ways = [len(tiles[j]) for j in early]
    late_ways = [len(tiles[j]) for j in late]
    half_shape = (rel_dev, width // 2, features)
    products = jax.ShapeDtypeStruct((len(early), slots, tile_rows, width), BF16)
    acc_scratch = pltpu.VMEM((per_tile + 1, tile_rows, features), F32)

    def call(body, operands, in_specs, out_shape, scratch, flops, aliases=None):
        return pl.pallas_call(
            body,
            out_shape=out_shape,
            in_specs=[SMEM] + in_specs,
            out_specs=[VMEM] * len(out_shape),
            scratch_shapes=scratch,
            input_output_aliases=aliases or {},
            cost_estimate=pl.CostEstimate(
                flops=flops, bytes_accessed=rel_dev * width * features, transcendentals=0
            ),
            compiler_params=pltpu.CompilerParams(vmem_limit_bytes=20 << 20),
        )(table, *operands)

    def message_shapes(count):
        shape = (ent_dev, own_features)
        one = [jax.ShapeDtypeStruct(shape, F32)] + [jax.ShapeDtypeStruct(shape, BF16)] * (n_rel - 1)
        return one * count

    slot_flops = 2 * slots * tile_rows * width
    flat = [t for j in early for t in tiles[j]]
    operands = [*states, *flat, *own_weights, *other_weights[0]]
    made, own_half, begun, rows_held = call(
        functools.partial(early_kernel, members, tuple(places), early_ways),
        operands,
        [HBM if v is values or v is rel_weight else ANY for v in operands],
        [
            products,
            jax.ShapeDtypeStruct(half_shape, BF16),
            jax.ShapeDtypeStruct(half_shape, BF16),
            jax.ShapeDtypeStruct((members * chunks, ent_dev, width), BF16),
        ],
        [
            pltpu.VMEM((len(early), slots, tile_rows, tile_rows), BF16),
            pltpu.SemaphoreType.DMA((len(states),)),
            pltpu.SemaphoreType.DMA((len(early),)),
            pltpu.SemaphoreType.DMA((members // 2,)),
            pltpu.SemaphoreType.DMA((members // 2,)),
        ],
        len(early) * slot_flops * tile_rows,
    )
    *two, other_half = call(
        functools.partial(first_kernel, members, 2, n_rel),
        [made, own_half, begun, *other_weights[1]],
        [VMEM] * 3 + [ANY] * (members // 2),
        message_shapes(1) + [jax.ShapeDtypeStruct(half_shape, BF16)],
        [acc_scratch, pltpu.SemaphoreType.DMA((members // 2,))],
        slot_flops * features,
        {3: n_rel},
    )
    results = {2: two}
    for j in (1, 0):
        results[j] = call(
            functools.partial(near_kernel, (j,), n_rel),
            [made, own_half, other_half],
            [VMEM] * 3,
            message_shapes(1),
            [acc_scratch],
            slot_flops * features,
        )
    flat = [t for j in late for t in tiles[j]]
    rest = call(
        functools.partial(late_kernel, members, late_ways, late, n_rel),
        [rows_held, own_half, other_half, *flat],
        [VMEM] * 3 + [ANY] * len(flat),
        message_shapes(len(late)),
        [
            pltpu.VMEM((len(late), slots, tile_rows, tile_rows), BF16),
            pltpu.VMEM((len(late), slots, tile_rows, width), BF16),
            acc_scratch,
            pltpu.SemaphoreType.DMA((len(late),)),
        ],
        len(late) * slot_flops * (features + tile_rows),
    )
    for g, j in enumerate(late):
        results[j] = rest[g * n_rel:(g + 1) * n_rel]

    def summed(j, dtype=BF16):
        moved = [swap(v, "rel", n_rel, r + 1) for r, v in enumerate(results[j][1:])]
        term = results[j][0]
        for other in moved:
            term = term + other.astype(F32)
        return term.astype(dtype)

    if line:
        passed = along(summed(2), [(0, 1), (1, 3), (3, 2), (2, 0)])
        three = lax.optimization_barrier(summed(3))
        across = along(three, [(0, 3), (3, 0)])
        total = (three.astype(F32) + passed.astype(F32)).astype(BF16)
        total = along(total, [(1, 2), (2, 1)])
        terms = [summed(0, F32), partner(summed(1), 1), across, total, passed]
        used = edge
    else:
        terms = [summed(0, F32)]
        terms += [partner(summed(j), j) for j in range(1, chunks)]
        used = jnp.ones((), jnp.int32)
    return pl.pallas_call(
        finish_kernel,
        out_shape=jax.ShapeDtypeStruct((ent_dev, own_features), BF16),
        in_specs=[SMEM] + [VMEM] * (3 + len(terms)),
        out_specs=VMEM,
        compiler_params=pltpu.CompilerParams(vmem_limit_bytes=12 << 20),
        name="finish",
    )(used.reshape(1), state, gate_open, update_bias[None], *terms)


def solution(mesh):
    n_rel, n_ent = mesh.shape["rel"], mesh.shape["ent"]
    chunks = max(4, n_rel)
    in_specs = (
        P("ent", "rel"),
        P("rel", "ent", None),
        P(None, "rel"),
        P("rel"),
        P("rel"),
        P("rel", "ent", None, None),
        P("rel", None, "ent"),
        P("rel", "ent"),
    )
    return jax.shard_map(
        functools.partial(shards, n_rel, n_ent, chunks),
        mesh=mesh, in_specs=in_specs, out_specs=P("ent", "rel"), check_vma=False,
    )
```
